32 devices in a mesh: tm: 8 (over z, x), chan: 4 (over y, core).
Axes of the slice: x: 2, y: 2, z: 4, core: 2. Of those that a mesh axis runs over, the one named last changes fastest.
Arguments:
- analysis_dep: bfloat16 [8, 1664, 2048], P('tm', 'chan')
- background_dep: bfloat16 [8, 1664, 2048], P('tm', 'chan')
- valid_counts: int32 [8], replicated, may hold values from 1 to 2048, as said below
Outputs:
- lag_covariance: float32 [1664, 5, 1664], P('tm', None, 'chan')
The draws below stay inside these ranges and needn't reach their ends.
Inputs may be any that keep to these rules, and one draw needn't show every extreme that they name: valid_counts of the last cycle is 2048.
All inputs are finite; a program needn't handle non-finite values.
Results may differ from the reference program's by a relative error of at most 0.0003.
Values may be sent and summed in bfloat16 or wider, within the bound.
No kernel may reach another device: no remote copies, remote signals or barrier semaphores. Data moves between devices by JAX's collectives and lax.ppermute only.
A program may use at most 128 MiB of HBM per device.

```python
import math
import jax
import jax.numpy as jnp

NCH = 1664
LOC = 2048
MAXLAG = 2
NLAGS = 5
NCYC = 8


def departures(key):
    base_key = jax.random.fold_in(key, 811)
    keys = jax.random.split(base_key, 4)
    dims = (NCYC, NCH, LOC)
    source = jax.random.normal(keys[0], dims, jnp.float32)
    fresh = jax.random.normal(keys[3], dims, jnp.float32)
    coupled = source + 0.5 * jnp.roll(source, 1, axis=1) + 0.25 * jnp.roll(source, -1, axis=1)
    zero_slab = jnp.zeros((1, NCH, LOC), jnp.float32)
    earlier_one = jnp.concatenate([zero_slab, coupled[:-1]], axis=0)
    earlier_two = jnp.concatenate([zero_slab, zero_slab, coupled[:-2]], axis=0)
    timed = coupled + 0.6 * earlier_one + 0.3 * earlier_two
    position = jnp.arange(LOC, dtype=jnp.float32) / LOC
    loc_scale = (0.3 + 2.7 * position)[None, None, :] * jnp.exp(jax.random.uniform(keys[1], (NCYC, 1, LOC), jnp.float32, -0.4, 0.4))
    chan_scale = jnp.exp(jax.random.uniform(keys[2], (1, NCH, 1), jnp.float32, math.log(0.3), math.log(3.0)))
    background = loc_scale * chan_scale * timed
    analysis = 0.5 * background + 0.5 * loc_scale * chan_scale * fresh
    return (analysis, background)


def draw_analysis_dep(key, part):
    return departures(key)[0].astype(jnp.bfloat16)


def draw_background_dep(key, part):
    return departures(key)[1].astype(jnp.bfloat16)


def draw_valid_counts(key, part):
    cycles = jnp.arange(NCYC, dtype=jnp.int32)
    lowest = LOC // 3
    ramp = lowest + cycles * (LOC - lowest) // (NCYC - 1)
    jitter = jax.random.randint(jax.random.fold_in(key, 29), (NCYC,), 0, LOC // 8 + 1)
    counted = jnp.where(cycles == NCYC - 1, LOC, ramp - jitter)
    return jnp.maximum(counted, 1).astype(jnp.int32)


def setup_inputs(seed: int = 0) -> dict:
    splits = jax.random.split(jax.random.key(seed), 4)
    analysis_dep = draw_analysis_dep(jax.random.fold_in(splits[3], 71), 0)
    background_dep = draw_background_dep(jax.random.fold_in(splits[3], 71), 0)
    valid_counts = draw_valid_counts(jax.random.fold_in(splits[3], 71), 0)
    return {"analysis_dep": analysis_dep, "background_dep": background_dep, "valid_counts": valid_counts}


def flatten(block):
    span = block.shape[0]
    return jnp.transpose(block, (1, 0, 2)).reshape(NCH, span * LOC)


def reference(analysis_dep, background_dep, valid_counts):
    positions = jnp.arange(LOC, dtype=jnp.int32)
    keep_rows = positions[None, :] < valid_counts[:, None]
    masked_analysis = jnp.where(keep_rows[:, None, :], analysis_dep, jnp.zeros((), analysis_dep.dtype))
    masked_background = jnp.where(keep_rows[:, None, :], background_dep, jnp.zeros((), background_dep.dtype))
    results = [None] * NLAGS
    for offset in range(MAXLAG + 1):
        span = NCYC - offset
        pairs = jnp.sum(jnp.minimum(valid_counts[:span], valid_counts[offset:])).astype(jnp.float32)
        later_b = flatten(masked_background[offset:])
        early_a = flatten(masked_analysis[:span])
        forward = jnp.dot(later_b, early_a.T, preferred_element_type=jnp.float32)
        results[MAXLAG + offset] = forward / pairs
        if offset > 0:
            early_b = flatten(masked_background[:span])
            later_a = flatten(masked_analysis[offset:])
            backward = jnp.dot(early_b, later_a.T, preferred_element_type=jnp.float32)
            results[MAXLAG - offset] = backward / pairs
    return jnp.stack(results, axis=1)
```

```python
import jax
import jax.numpy as jnp
from jax import lax
from jax.sharding import PartitionSpec as P


def contract(left, right):
    return lax.dot_general(
        left, right, (((0, 2), (0, 2)), ((), ())), preferred_element_type=jnp.float32
    )


def body(analysis_dep, background_dep, valid_counts):
    cycle_total = valid_counts.shape[0]
    tm_size = lax.axis_size("tm")
    chan_size = lax.axis_size("chan")
    lag_total = 5
    max_lag = (lag_total - 1) // 2
    cycle_index = lax.axis_index("tm")
    own_count = jnp.sum(
        jnp.where(jnp.arange(cycle_total, dtype=jnp.int32) == cycle_index, valid_counts, 0)
    )
    _, width_block, loc_total = analysis_dep.shape
    chan_total = width_block * chan_size
    row_block = chan_total // tm_size
    valid_cols = (jnp.arange(loc_total, dtype=jnp.int32) < own_count)[None, :]
    local_analysis = jnp.where(valid_cols, analysis_dep[0], jnp.zeros((), jnp.bfloat16))
    local_background = jnp.where(valid_cols, background_dep[0], jnp.zeros((), jnp.bfloat16))

    all_analysis = lax.all_gather(local_analysis, "tm", axis=0, tiled=False)

    by_loc = lax.all_to_all(local_background, "chan", 1, 0, tiled=True)
    by_loc = by_loc.reshape(tm_size, row_block, loc_total // chan_size)
    rows_here = lax.all_to_all(by_loc, "tm", 0, 0, tiled=True)
    all_background = lax.all_gather(rows_here, "chan", axis=2, tiled=True)

    pieces = [None] * lag_total
    for offset in range(max_lag + 1):
        span = cycle_total - offset
        pairs = jnp.sum(jnp.minimum(valid_counts[:span], valid_counts[offset:])).astype(jnp.float32)
        forward = contract(all_background[offset:], all_analysis[:span])
        pieces[max_lag + offset] = forward / pairs
        if offset > 0:
            backward = contract(all_background[:span], all_analysis[offset:])
            pieces[max_lag - offset] = backward / pairs
    return jnp.stack(pieces, axis=1)


def solution(mesh):
    in_specs = (P("tm", "chan", None), P("tm", "chan", None), P())
    out_specs = P("tm", None, "chan")
    return jax.shard_map(body, mesh=mesh, in_specs=in_specs, out_specs=out_specs, check_vma=False)
```

```python
import jax
import jax.numpy as jnp
from jax import lax
from jax.sharding import Mesh, PartitionSpec as P

PAIR = 2


def contract(left, right):
    return lax.dot_general(
        left, right, (((0, 2), (0, 2)), ((), ())), preferred_element_type=jnp.float32
    )


def body(analysis_dep, background_dep, valid_counts):
    cycle_total = valid_counts.shape[0]
    quad_size = lax.axis_size("tq")
    chan_size = lax.axis_size("chan")
    lag_total = 5
    max_lag = (lag_total - 1) // 2
    cycle_index = lax.axis_index("tq") * PAIR + lax.axis_index("th")
    own_count = jnp.sum(
        jnp.where(jnp.arange(cycle_total, dtype=jnp.int32) == cycle_index, valid_counts, 0)
    )
    _, width_block, loc_total = analysis_dep.shape
    half = loc_total // PAIR
    piece = half // chan_size
    pair_rows = width_block * chan_size // quad_size
    valid_cols = (jnp.arange(loc_total, dtype=jnp.int32) < own_count)[None, :]
    local_analysis = jnp.where(valid_cols, analysis_dep[0], jnp.zeros((), jnp.bfloat16))
    local_background = jnp.where(valid_cols, background_dep[0], jnp.zeros((), jnp.bfloat16))

    halves = local_analysis.reshape(width_block, PAIR, half).transpose(1, 0, 2)
    pair_analysis = lax.all_to_all(halves, "th", 0, 0, tiled=True)
    all_analysis = lax.all_gather(pair_analysis, "tq", axis=0, tiled=True)

    split_b = local_background.reshape(width_block, PAIR, chan_size, piece)
    by_loc = lax.all_to_all(split_b, "chan", 2, 0, tiled=True)
    by_loc = by_loc.reshape(quad_size, pair_rows, PAIR, piece).transpose(0, 2, 1, 3)
    by_loc = by_loc.reshape(quad_size * PAIR, pair_rows, piece)
    rows_here = lax.all_to_all(by_loc, ("tq", "th"), 0, 0, tiled=True)
    all_background = lax.all_gather(rows_here, "chan", axis=2, tiled=True)

    pieces = [None] * lag_total
    for offset in range(max_lag + 1):
        span = cycle_total - offset
        pieces[max_lag + offset] = contract(all_background[offset:], all_analysis[:span])
        if offset > 0:
            pieces[max_lag - offset] = contract(all_background[:span], all_analysis[offset:])
    partial = jnp.stack(pieces, axis=1)
    summed = lax.psum_scatter(partial, "th", scatter_dimension=0, tiled=True)

    denominators = []
    for offset in range(max_lag + 1):
        span = cycle_total - offset
        denominators.append(
            jnp.sum(jnp.minimum(valid_counts[:span], valid_counts[offset:])).astype(jnp.float32)
        )
    divisor = jnp.stack([denominators[abs(k - max_lag)] for k in range(lag_total)])
    return summed / divisor[None, :, None]


def solution(mesh):
    tm_size, chan_size = mesh.devices.shape
    split = Mesh(mesh.devices.reshape(tm_size // PAIR, PAIR, chan_size), ("tq", "th", "chan"))
    in_specs = (P(("tq", "th"), "chan", None), P(("tq", "th"), "chan", None), P())
    out_specs = P(("tq", "th"), None, "chan")
    return jax.shard_map(body, mesh=split, in_specs=in_specs, out_specs=out_specs, check_vma=False)
```

```python
import jax
import jax.numpy as jnp
from jax import lax
from jax.sharding import Mesh, PartitionSpec as P

PAIR = 2


def swap_pair(x):
    return lax.ppermute(x, "th", [(0, 1), (1, 0)])


def gather_chan(x, axis):
    size = lax.axis_size("chan")
    me = lax.axis_index("chan")
    bits = size.bit_length() - 1
    held = x
    for done, bit in enumerate(reversed(range(bits))):
        got = lax.ppermute(held, "chan", [(c, c ^ (1 << bit)) for c in range(size)])
        low = ((me >> bit) & 1) == 0
        first = jnp.where(low, held, got)
        second = jnp.where(low, got, held)
        held = jnp.stack([first, second], axis=axis + done)
    shape = list(x.shape)
    shape[axis] *= size
    return held.reshape(shape)


def contract(left, right):
    return lax.dot_general(
        left, right, (((0, 2), (0, 2)), ((), ())), preferred_element_type=jnp.float32
    )


def body(analysis_dep, background_dep, valid_counts):
    cycle_total = valid_counts.shape[0]
    quad_size = lax.axis_size("tq")
    chan_size = lax.axis_size("chan")
    lag_total = 5
    max_lag = (lag_total - 1) // 2
    cycle_index = lax.axis_index("tq") * PAIR + lax.axis_index("th")
    own_count = jnp.sum(
        jnp.where(jnp.arange(cycle_total, dtype=jnp.int32) == cycle_index, valid_counts, 0)
    )
    _, width_block, loc_total = analysis_dep.shape
    half = loc_total // PAIR
    piece = half // chan_size
    pair_rows = width_block * chan_size // quad_size
    valid_cols = (jnp.arange(loc_total, dtype=jnp.int32) < own_count)[None, :]
    local_analysis = jnp.where(valid_cols, analysis_dep[0], jnp.zeros((), jnp.bfloat16))
    local_background = jnp.where(valid_cols, background_dep[0], jnp.zeros((), jnp.bfloat16))

    pair_index = lax.axis_index("th")
    halves = local_analysis.reshape(width_block, PAIR, half)
    keep = jnp.where(pair_index == 0, halves[:, 0], halves[:, 1])
    give = jnp.where(pair_index == 0, halves[:, 1], halves[:, 0])
    got = swap_pair(give)
    pair_analysis = jnp.where(pair_index == 0, jnp.stack([keep, got]), jnp.stack([got, keep]))
    all_analysis = lax.all_gather(pair_analysis, "tq", axis=0, tiled=True)

    split_b = local_background.reshape(width_block, PAIR, chan_size, piece)
    by_loc = lax.all_to_all(split_b, "chan", 2, 0, tiled=True)
    by_loc = by_loc.reshape(quad_size, pair_rows, PAIR, piece).transpose(0, 2, 1, 3)
    by_loc = by_loc.reshape(quad_size * PAIR, pair_rows, piece)
    rows_here = lax.all_to_all(by_loc, ("tq", "th"), 0, 0, tiled=True)
    all_background = gather_chan(rows_here, 2)

    pieces = [None] * lag_total
    for offset in range(max_lag + 1):
        span = cycle_total - offset
        pieces[max_lag + offset] = contract(all_background[offset:], all_analysis[:span])
        if offset > 0:
            pieces[max_lag - offset] = contract(all_background[:span], all_analysis[offset:])
    partial = jnp.stack(pieces, axis=1)
    rows_out = partial.shape[0] // PAIR
    upper = jnp.where(pair_index == 0, partial[rows_out:], partial[:rows_out])
    lower = jnp.where(pair_index == 0, partial[:rows_out], partial[rows_out:])
    summed = lower + swap_pair(upper)

    denominators = []
    for offset in range(max_lag + 1):
        span = cycle_total - offset
        denominators.append(
            jnp.sum(jnp.minimum(valid_counts[:span], valid_counts[offset:])).astype(jnp.float32)
        )
    divisor = jnp.stack([denominators[abs(k - max_lag)] for k in range(lag_total)])
    return summed / divisor[None, :, None]


def solution(mesh):
    tm_size, chan_size = mesh.devices.shape
    split = Mesh(mesh.devices.reshape(tm_size // PAIR, PAIR, chan_size), ("tq", "th", "chan"))
    in_specs = (P(("tq", "th"), "chan", None), P(("tq", "th"), "chan", None), P())
    out_specs = P(("tq", "th"), None, "chan")
    return jax.shard_map(body, mesh=split, in_specs=in_specs, out_specs=out_specs, check_vma=False)
```

```python
import jax
import jax.numpy as jnp
from jax import lax
from jax.sharding import Mesh, PartitionSpec as P

PAIR = 2


def swap_pair(x):
    return lax.ppermute(x, "th", [(0, 1), (1, 0)])


def contract(left, right):
    return lax.dot_general(
        left, right, (((0, 2), (0, 2)), ((), ())), preferred_element_type=jnp.float32
    )


def body(analysis_dep, background_dep, valid_counts):
    cycle_total = valid_counts.shape[0]
    quad_size = lax.axis_size("tq")
    chan_size = lax.axis_size("chan")
    lag_total = 5
    max_lag = (lag_total - 1) // 2
    cycle_index = lax.axis_index("tq") * PAIR + lax.axis_index("th")
    own_count = jnp.sum(
        jnp.where(jnp.arange(cycle_total, dtype=jnp.int32) == cycle_index, valid_counts, 0)
    )
    _, width_block, loc_total = analysis_dep.shape
    half = loc_total // PAIR
    piece = half // chan_size
    pair_rows = width_block * chan_size // quad_size
    valid_cols = (jnp.arange(loc_total, dtype=jnp.int32) < own_count)[None, :]
    local_analysis = jnp.where(valid_cols, analysis_dep[0], jnp.zeros((), jnp.bfloat16))
    local_background = jnp.where(valid_cols, background_dep[0], jnp.zeros((), jnp.bfloat16))

    pair_index = lax.axis_index("th")
    halves = local_analysis.reshape(width_block, PAIR, half)
    keep = jnp.where(pair_index == 0, halves[:, 0], halves[:, 1])
    give = jnp.where(pair_index == 0, halves[:, 1], halves[:, 0])
    got = swap_pair(give)
    pair_analysis = jnp.where(pair_index == 0, jnp.stack([keep, got]), jnp.stack([got, keep]))
    all_analysis = lax.all_gather(pair_analysis, "tq", axis=0, tiled=True)

    split_b = local_background.reshape(width_block, PAIR, chan_size, piece)
    by_loc = lax.all_to_all(split_b, "chan", 2, 0, tiled=True)
    by_loc = by_loc.reshape(quad_size, pair_rows, PAIR, piece).transpose(0, 2, 1, 3)
    by_loc = by_loc.reshape(quad_size * PAIR, pair_rows, piece)
    rows_here = lax.all_to_all(by_loc, ("tq", "th"), 0, 0, tiled=True)
    all_background = lax.all_gather(rows_here, "chan", axis=2, tiled=True)

    pieces = [None] * lag_total
    for offset in range(max_lag + 1):
        span = cycle_total - offset
        pieces[max_lag + offset] = contract(all_background[offset:], all_analysis[:span])
        if offset > 0:
            pieces[max_lag - offset] = contract(all_background[:span], all_analysis[offset:])
    partial = jnp.stack(pieces, axis=1)
    rows_out = partial.shape[0] // PAIR
    upper = jnp.where(pair_index == 0, partial[rows_out:], partial[:rows_out])
    lower = jnp.where(pair_index == 0, partial[:rows_out], partial[rows_out:])
    summed = lower + swap_pair(upper)

    denominators = []
    for offset in range(max_lag + 1):
        span = cycle_total - offset
        denominators.append(
            jnp.sum(jnp.minimum(valid_counts[:span], valid_counts[offset:])).astype(jnp.float32)
        )
    divisor = jnp.stack([denominators[abs(k - max_lag)] for k in range(lag_total)])
    return summed / divisor[None, :, None]


def solution(mesh):
    tm_size, chan_size = mesh.devices.shape
    split = Mesh(mesh.devices.reshape(tm_size // PAIR, PAIR, chan_size), ("tq", "th", "chan"))
    in_specs = (P(("tq", "th"), "chan", None), P(("tq", "th"), "chan", None), P())
    out_specs = P(("tq", "th"), None, "chan")
    return jax.shard_map(body, mesh=split, in_specs=in_specs, out_specs=out_specs, check_vma=False)
```

```python
import jax
import jax.numpy as jnp
from jax import lax
from jax.sharding import Mesh, PartitionSpec as P

PAIR = 2


def swap_pair(x):
    return lax.ppermute(x, "th", [(0, 1), (1, 0)])


def gather_chan(x):
    size = lax.axis_size("chan")
    me = lax.axis_index("chan")
    bits = size.bit_length() - 1
    held = x[None]
    for bit in reversed(range(bits)):
        got = lax.ppermute(held, "chan", [(c, c ^ (1 << bit)) for c in range(size)])
        low = ((me >> bit) & 1) == 0
        first = jnp.where(low, held, got)
        second = jnp.where(low, got, held)
        held = jnp.concatenate([first, second], axis=0) if bit == bits - 1 else jnp.stack([first, second], axis=1).reshape((-1,) + x.shape)
    return held


def contract(left, right):
    return lax.dot_general(
        left, right, (((0, 1, 3), (0, 1, 3)), ((), ())), preferred_element_type=jnp.float32
    )


def lag_block(background, analysis, cycle_total, max_lag, lag_total):
    pieces = [None] * lag_total
    for offset in range(max_lag + 1):
        span = cycle_total - offset
        pieces[max_lag + offset] = contract(background[:, offset:], analysis[:, :span])
        if offset > 0:
            pieces[max_lag - offset] = contract(background[:, :span], analysis[:, offset:])
    return jnp.stack(pieces, axis=1)


def body(analysis_dep, background_dep, valid_counts):
    cycle_total = valid_counts.shape[0]
    quad_size = lax.axis_size("tq")
    chan_size = lax.axis_size("chan")
    lag_total = 5
    max_lag = (lag_total - 1) // 2
    pair_index = lax.axis_index("th")
    cycle_index = lax.axis_index("tq") * PAIR + pair_index
    own_count = jnp.sum(
        jnp.where(jnp.arange(cycle_total, dtype=jnp.int32) == cycle_index, valid_counts, 0)
    )
    _, width_block, loc_total = analysis_dep.shape
    half = loc_total // PAIR
    piece = half // chan_size
    pair_rows = width_block * chan_size // quad_size
    valid_cols = (jnp.arange(loc_total, dtype=jnp.int32) < own_count)[None, :]
    local_analysis = jnp.where(valid_cols, analysis_dep[0], jnp.zeros((), jnp.bfloat16))
    local_background = jnp.where(valid_cols, background_dep[0], jnp.zeros((), jnp.bfloat16))

    halves = local_analysis.reshape(width_block, PAIR, half)
    keep = jnp.where(pair_index == 0, halves[:, 0], halves[:, 1])
    give = jnp.where(pair_index == 0, halves[:, 1], halves[:, 0])
    got = swap_pair(give)
    pair_analysis = jnp.where(pair_index == 0, jnp.stack([keep, got]), jnp.stack([got, keep]))
    pair_analysis = pair_analysis.reshape(PAIR, width_block, chan_size, piece).transpose(2, 0, 1, 3)
    all_analysis = lax.all_gather(pair_analysis, "tq", axis=1, tiled=True)

    split_b = local_background.reshape(width_block, PAIR, chan_size, piece)
    by_loc = lax.all_to_all(split_b, "chan", 2, 0, tiled=True)
    by_loc = by_loc.reshape(quad_size, pair_rows, PAIR, piece).transpose(0, 2, 1, 3)
    by_loc = by_loc.reshape(quad_size * PAIR, pair_rows, piece)
    rows_here = lax.all_to_all(by_loc, ("tq", "th"), 0, 0, tiled=True)
    all_background = gather_chan(rows_here)

    rows_out = pair_rows // PAIR
    give_rows = lax.dynamic_slice_in_dim(all_background, (1 - pair_index) * rows_out, rows_out, axis=2)
    keep_rows = lax.dynamic_slice_in_dim(all_background, pair_index * rows_out, rows_out, axis=2)
    sent = swap_pair(lag_block(give_rows, all_analysis, cycle_total, max_lag, lag_total))
    summed = lag_block(keep_rows, all_analysis, cycle_total, max_lag, lag_total) + sent

    denominators = []
    for offset in range(max_lag + 1):
        span = cycle_total - offset
        denominators.append(
            jnp.sum(jnp.minimum(valid_counts[:span], valid_counts[offset:])).astype(jnp.float32)
        )
    divisor = jnp.stack([denominators[abs(k - max_lag)] for k in range(lag_total)])
    return summed / divisor[None, :, None]


def solution(mesh):
    tm_size, chan_size = mesh.devices.shape
    split = Mesh(mesh.devices.reshape(tm_size // PAIR, PAIR, chan_size), ("tq", "th", "chan"))
    in_specs = (P(("tq", "th"), "chan", None), P(("tq", "th"), "chan", None), P())
    out_specs = P(("tq", "th"), None, "chan")
    return jax.shard_map(body, mesh=split, in_specs=in_specs, out_specs=out_specs, check_vma=False)
```

```python
import jax
import jax.numpy as jnp
from jax import lax
from jax.sharding import Mesh, PartitionSpec as P

PAIR = 2


def swap_pair(x):
    return lax.ppermute(x, "th", [(0, 1), (1, 0)])


def gather_chan(x):
    size = lax.axis_size("chan")
    me = lax.axis_index("chan")
    bits = size.bit_length() - 1
    held = x[None]
    for bit in reversed(range(bits)):
        got = lax.ppermute(held, "chan", [(c, c ^ (1 << bit)) for c in range(size)])
        low = ((me >> bit) & 1) == 0
        first = jnp.where(low, held, got)
        second = jnp.where(low, got, held)
        held = jnp.concatenate([first, second], axis=0) if bit == bits - 1 else jnp.stack([first, second], axis=1).reshape((-1,) + x.shape)
    return held


def contract(left, right):
    return lax.dot_general(
        left, right, (((0, 1, 3), (0, 1, 3)), ((), ())), preferred_element_type=jnp.float32
    )


def lag_block(background, analysis, cycle_total, max_lag, lag_total):
    pieces = [None] * lag_total
    for offset in range(max_lag + 1):
        span = cycle_total - offset
        pieces[max_lag + offset] = contract(background[:, offset:], analysis[:, :span])
        if offset > 0:
            pieces[max_lag - offset] = contract(background[:, :span], analysis[:, offset:])
    return jnp.stack(pieces, axis=1)


def body(analysis_dep, background_dep, valid_counts):
    cycle_total = valid_counts.shape[0]
    quad_size = lax.axis_size("tq")
    chan_size = lax.axis_size("chan")
    lag_total = 5
    max_lag = (lag_total - 1) // 2
    pair_index = lax.axis_index("th")
    cycle_index = lax.axis_index("tq") * PAIR + pair_index
    own_count = jnp.sum(
        jnp.where(jnp.arange(cycle_total, dtype=jnp.int32) == cycle_index, valid_counts, 0)
    )
    _, width_block, loc_total = analysis_dep.shape
    half = loc_total // PAIR
    piece = half // chan_size
    pair_rows = width_block * chan_size // quad_size
    valid_cols = (jnp.arange(loc_total, dtype=jnp.int32) < own_count)[None, :]
    local_analysis = jnp.where(valid_cols, analysis_dep[0], jnp.zeros((), jnp.bfloat16))
    local_background = jnp.where(valid_cols, background_dep[0], jnp.zeros((), jnp.bfloat16))

    halves = local_analysis.reshape(width_block, PAIR, half)
    keep = jnp.where(pair_index == 0, halves[:, 0], halves[:, 1])
    give = jnp.where(pair_index == 0, halves[:, 1], halves[:, 0])
    def by_piece(x):
        return x.reshape(width_block, chan_size, piece).transpose(1, 0, 2)[:, None]

    same_parity = lax.all_gather(by_piece(keep), "tq", axis=1, tiled=True)
    got = swap_pair(give)
    other_parity = lax.all_gather(by_piece(got), "tq", axis=1, tiled=True)
    even = jnp.where(pair_index == 0, same_parity, other_parity)
    odd = jnp.where(pair_index == 0, other_parity, same_parity)
    all_analysis = jnp.stack([even, odd], axis=2).reshape(chan_size, cycle_total, width_block, piece)

    split_b = local_background.reshape(width_block, PAIR, chan_size, piece)
    by_loc = lax.all_to_all(split_b, "chan", 2, 0, tiled=True)
    by_loc = by_loc.reshape(quad_size, pair_rows, PAIR, piece).transpose(0, 2, 1, 3)
    by_loc = by_loc.reshape(quad_size * PAIR, pair_rows, piece)
    rows_here = lax.all_to_all(by_loc, ("tq", "th"), 0, 0, tiled=True)
    all_background = gather_chan(rows_here)

    rows_out = pair_rows // PAIR
    give_rows = lax.dynamic_slice_in_dim(all_background, (1 - pair_index) * rows_out, rows_out, axis=2)
    keep_rows = lax.dynamic_slice_in_dim(all_background, pair_index * rows_out, rows_out, axis=2)
    sent = swap_pair(lag_block(give_rows, all_analysis, cycle_total, max_lag, lag_total))
    summed = lag_block(keep_rows, all_analysis, cycle_total, max_lag, lag_total) + sent

    denominators = []
    for offset in range(max_lag + 1):
        span = cycle_total - offset
        denominators.append(
            jnp.sum(jnp.minimum(valid_counts[:span], valid_counts[offset:])).astype(jnp.float32)
        )
    divisor = jnp.stack([denominators[abs(k - max_lag)] for k in range(lag_total)])
    return summed / divisor[None, :, None]


def solution(mesh):
    tm_size, chan_size = mesh.devices.shape
    split = Mesh(mesh.devices.reshape(tm_size // PAIR, PAIR, chan_size), ("tq", "th", "chan"))
    in_specs = (P(("tq", "th"), "chan", None), P(("tq", "th"), "chan", None), P())
    out_specs = P(("tq", "th"), None, "chan")
    return jax.shard_map(body, mesh=split, in_specs=in_specs, out_specs=out_specs, check_vma=False)
```

```python
import jax
import jax.numpy as jnp
from jax import lax
from jax.sharding import Mesh, PartitionSpec as P

PAIR = 2


def swap_pair(x):
    return lax.ppermute(x, "th", [(0, 1), (1, 0)])


def gather_chan(x):
    size = lax.axis_size("chan")
    me = lax.axis_index("chan")
    bits = size.bit_length() - 1
    held = x[None]
    for bit in reversed(range(bits)):
        got = lax.ppermute(held, "chan", [(c, c ^ (1 << bit)) for c in range(size)])
        low = ((me >> bit) & 1) == 0
        first = jnp.where(low, held, got)
        second = jnp.where(low, got, held)
        held = jnp.concatenate([first, second], axis=0) if bit == bits - 1 else jnp.stack([first, second], axis=1).reshape((-1,) + x.shape)
    return held


def contract(left, right):
    return lax.dot_general(
        left, right, (((0, 1, 3), (0, 1, 3)), ((), ())), preferred_element_type=jnp.float32
    )


def lag_block(shifted, even, odd, max_lag, lag_total):
    pieces = []
    for k in range(lag_total):
        lag = k - max_lag
        pieces.append(contract(shifted(lag), even) + contract(shifted(lag + 1), odd))
    return jnp.stack(pieces, axis=1)


def body(analysis_dep, background_dep, valid_counts):
    cycle_total = valid_counts.shape[0]
    quad_size = lax.axis_size("tq")
    chan_size = lax.axis_size("chan")
    lag_total = 5
    max_lag = (lag_total - 1) // 2
    pair_index = lax.axis_index("th")
    cycle_index = lax.axis_index("tq") * PAIR + pair_index
    own_count = jnp.sum(
        jnp.where(jnp.arange(cycle_total, dtype=jnp.int32) == cycle_index, valid_counts, 0)
    )
    _, width_block, loc_total = analysis_dep.shape
    half = loc_total // PAIR
    piece = half // chan_size
    pair_rows = width_block * chan_size // quad_size
    valid_cols = (jnp.arange(loc_total, dtype=jnp.int32) < own_count)[None, :]
    local_analysis = jnp.where(valid_cols, analysis_dep[0], jnp.zeros((), jnp.bfloat16))
    local_background = jnp.where(valid_cols, background_dep[0], jnp.zeros((), jnp.bfloat16))

    halves = local_analysis.reshape(width_block, PAIR, half)
    keep = jnp.where(pair_index == 0, halves[:, 0], halves[:, 1])
    give = jnp.where(pair_index == 0, halves[:, 1], halves[:, 0])
    def by_piece(x):
        return x.reshape(width_block, chan_size, piece).transpose(1, 0, 2)[:, None]

    same_parity = lax.all_gather(by_piece(keep), "tq", axis=1, tiled=True)
    got = swap_pair(give)
    other_parity = lax.all_gather(by_piece(got), "tq", axis=1, tiled=True)
    even = jnp.where(pair_index == 0, same_parity, other_parity)
    odd = jnp.where(pair_index == 0, other_parity, same_parity)

    split_b = local_background.reshape(width_block, PAIR, chan_size, piece)
    by_loc = lax.all_to_all(split_b, "chan", 2, 0, tiled=True)
    by_loc = by_loc.reshape(quad_size, pair_rows, PAIR, piece).transpose(0, 2, 1, 3)
    rows_out = pair_rows // PAIR
    by_loc = by_loc.reshape(quad_size, PAIR, PAIR, rows_out, piece)
    by_loc = jnp.stack([by_loc[:, 0], by_loc[:, 1, ::-1]], axis=1)
    by_loc = by_loc.reshape(quad_size * PAIR, pair_rows, piece)
    rows_here = lax.all_to_all(by_loc, ("tq", "th"), 0, 0, tiled=True)
    all_background = gather_chan(rows_here)
    by_parity = all_background.reshape(chan_size, quad_size, PAIR, pair_rows, piece).transpose(0, 2, 1, 3, 4)
    padded = jnp.pad(by_parity, ((0, 0), (0, 0), (1, 1), (0, 0), (0, 0)))

    def own_rows(lag):
        start = 1 + lag // 2
        return padded[:, lag % 2, start:start + quad_size, :rows_out]

    def partner_rows(lag):
        start = 1 + lag // 2
        return padded[:, lag % 2, start:start + quad_size, rows_out:]

    sent = swap_pair(lag_block(partner_rows, even, odd, max_lag, lag_total))
    summed = lag_block(own_rows, even, odd, max_lag, lag_total) + sent

    denominators = []
    for offset in range(max_lag + 1):
        span = cycle_total - offset
        denominators.append(
            jnp.sum(jnp.minimum(valid_counts[:span], valid_counts[offset:])).astype(jnp.float32)
        )
    divisor = jnp.stack([denominators[abs(k - max_lag)] for k in range(lag_total)])
    return summed / divisor[None, :, None]


def solution(mesh):
    tm_size, chan_size = mesh.devices.shape
    split = Mesh(mesh.devices.reshape(tm_size // PAIR, PAIR, chan_size), ("tq", "th", "chan"))
    in_specs = (P(("tq", "th"), "chan", None), P(("tq", "th"), "chan", None), P())
    out_specs = P(("tq", "th"), None, "chan")
    return jax.shard_map(body, mesh=split, in_specs=in_specs, out_specs=out_specs, check_vma=False)
```

```python
import jax
import jax.numpy as jnp
from jax import lax
from jax.sharding import Mesh, PartitionSpec as P

PAIR = 2


def swap_pair(x):
    return lax.ppermute(x, "th", [(0, 1), (1, 0)])


def gather_chan(x):
    size = lax.axis_size("chan")
    me = lax.axis_index("chan")
    bits = size.bit_length() - 1
    held = x[None]
    for bit in reversed(range(bits)):
        got = lax.ppermute(held, "chan", [(c, c ^ (1 << bit)) for c in range(size)])
        low = ((me >> bit) & 1) == 0
        first = jnp.where(low, held, got)
        second = jnp.where(low, got, held)
        held = jnp.concatenate([first, second], axis=0) if bit == bits - 1 else jnp.stack([first, second], axis=1).reshape((-1,) + x.shape)
    return held


def contract(left, right):
    return lax.dot_general(
        left, right, (((0, 1, 3), (0, 1, 3)), ((), ())), preferred_element_type=jnp.float32
    )


def lag_block(background, analysis, cycle_total, max_lag, lags):
    pieces = []
    for k in lags:
        offset = k - max_lag
        if offset >= 0:
            span = cycle_total - offset
            pieces.append(contract(background[:, offset:], analysis[:, :span]))
        else:
            span = cycle_total + offset
            pieces.append(contract(background[:, :span], analysis[:, -offset:]))
    return jnp.stack(pieces, axis=1)


def body(analysis_dep, background_dep, valid_counts):
    cycle_total = valid_counts.shape[0]
    quad_size = lax.axis_size("tq")
    chan_size = lax.axis_size("chan")
    lag_total = 5
    max_lag = (lag_total - 1) // 2
    pair_index = lax.axis_index("th")
    cycle_index = lax.axis_index("tq") * PAIR + pair_index
    own_count = jnp.sum(
        jnp.where(jnp.arange(cycle_total, dtype=jnp.int32) == cycle_index, valid_counts, 0)
    )
    _, width_block, loc_total = analysis_dep.shape
    half = loc_total // PAIR
    piece = half // chan_size
    pair_rows = width_block * chan_size // quad_size
    valid_cols = (jnp.arange(loc_total, dtype=jnp.int32) < own_count)[None, :]
    local_analysis = jnp.where(valid_cols, analysis_dep[0], jnp.zeros((), jnp.bfloat16))
    local_background = jnp.where(valid_cols, background_dep[0], jnp.zeros((), jnp.bfloat16))

    halves = local_analysis.reshape(width_block, PAIR, half)
    keep = jnp.where(pair_index == 0, halves[:, 0], halves[:, 1])
    give = jnp.where(pair_index == 0, halves[:, 1], halves[:, 0])
    got = swap_pair(give)
    pair_analysis = jnp.where(pair_index == 0, jnp.stack([keep, got]), jnp.stack([got, keep]))
    pair_analysis = pair_analysis.reshape(PAIR, width_block, chan_size, piece).transpose(2, 0, 1, 3)
    all_analysis = lax.all_gather(pair_analysis, "tq", axis=1, tiled=True)

    split_b = local_background.reshape(width_block, PAIR, chan_size, piece)
    by_loc = lax.all_to_all(split_b, "chan", 2, 0, tiled=True)
    by_loc = by_loc.reshape(quad_size, pair_rows, PAIR, piece).transpose(0, 2, 1, 3)
    rows_out = pair_rows // PAIR
    by_loc = by_loc.reshape(quad_size, PAIR, PAIR, rows_out, piece)
    by_loc = jnp.stack([by_loc[:, 0], by_loc[:, 1, ::-1]], axis=1)
    by_loc = by_loc.reshape(quad_size * PAIR, pair_rows, piece)
    rows_here = lax.all_to_all(by_loc, ("tq", "th"), 0, 0, tiled=True)
    all_background = gather_chan(rows_here)

    keep_rows = all_background[:, :, :rows_out]
    give_rows = all_background[:, :, rows_out:]
    early = (0, 1)
    late = tuple(k for k in range(lag_total) if k not in early)
    sent_early = swap_pair(lag_block(give_rows, all_analysis, cycle_total, max_lag, early))
    sent_late = swap_pair(lag_block(give_rows, all_analysis, cycle_total, max_lag, late))
    own = lag_block(keep_rows, all_analysis, cycle_total, max_lag, tuple(range(lag_total)))
    summed = own + jnp.concatenate([sent_early, sent_late], axis=1)

    denominators = []
    for offset in range(max_lag + 1):
        span = cycle_total - offset
        denominators.append(
            jnp.sum(jnp.minimum(valid_counts[:span], valid_counts[offset:])).astype(jnp.float32)
        )
    divisor = jnp.stack([denominators[abs(k - max_lag)] for k in range(lag_total)])
    return summed / divisor[None, :, None]


def solution(mesh):
    tm_size, chan_size = mesh.devices.shape
    split = Mesh(mesh.devices.reshape(tm_size // PAIR, PAIR, chan_size), ("tq", "th", "chan"))
    in_specs = (P(("tq", "th"), "chan", None), P(("tq", "th"), "chan", None), P())
    out_specs = P(("tq", "th"), None, "chan")
    return jax.shard_map(body, mesh=split, in_specs=in_specs, out_specs=out_specs, check_vma=False)
```

```python
import jax
import jax.numpy as jnp
from jax import lax
from jax.sharding import Mesh, PartitionSpec as P

PAIR = 2


def swap_pair(x):
    return lax.ppermute(x, "th", [(0, 1), (1, 0)])


def gather_chan(x):
    size = lax.axis_size("chan")
    me = lax.axis_index("chan")
    bits = size.bit_length() - 1
    held = x[None]
    for bit in reversed(range(bits)):
        got = lax.ppermute(held, "chan", [(c, c ^ (1 << bit)) for c in range(size)])
        low = ((me >> bit) & 1) == 0
        first = jnp.where(low, held, got)
        second = jnp.where(low, got, held)
        held = jnp.concatenate([first, second], axis=0) if bit == bits - 1 else jnp.stack([first, second], axis=1).reshape((-1,) + x.shape)
    return held


def relay_gather(block, size):
    me = lax.axis_index("tq")
    from_left = from_right = block
    lefts, rights = [], []
    for _ in range(size - 1):
        from_left = lax.ppermute(from_left, "tq", [(i, i + 1) for i in range(size - 1)])
        from_right = lax.ppermute(from_right, "tq", [(i + 1, i) for i in range(size - 1)])
        lefts.append(from_left)
        rights.append(from_right)
    stacked = jnp.concatenate(lefts[::-1] + [block] + rights, axis=1)
    width = block.shape[1]
    return lax.dynamic_slice_in_dim(stacked, (size - 1 - me) * width, size * width, axis=1)


def contract(left, right):
    return lax.dot_general(
        left, right, (((0, 1, 3), (0, 1, 3)), ((), ())), preferred_element_type=jnp.float32
    )


def lag_block(background, analysis, cycle_total, max_lag, lag_total):
    pieces = [None] * lag_total
    for offset in range(max_lag + 1):
        span = cycle_total - offset
        pieces[max_lag + offset] = contract(background[:, offset:], analysis[:, :span])
        if offset > 0:
            pieces[max_lag - offset] = contract(background[:, :span], analysis[:, offset:])
    return jnp.stack(pieces, axis=1)


def body(analysis_dep, background_dep, valid_counts):
    cycle_total = valid_counts.shape[0]
    quad_size = lax.axis_size("tq")
    chan_size = lax.axis_size("chan")
    lag_total = 5
    max_lag = (lag_total - 1) // 2
    pair_index = lax.axis_index("th")
    cycle_index = lax.axis_index("tq") * PAIR + pair_index
    own_count = jnp.sum(
        jnp.where(jnp.arange(cycle_total, dtype=jnp.int32) == cycle_index, valid_counts, 0)
    )
    _, width_block, loc_total = analysis_dep.shape
    half = loc_total // PAIR
    piece = half // chan_size
    pair_rows = width_block * chan_size // quad_size
    valid_cols = (jnp.arange(loc_total, dtype=jnp.int32) < own_count)[None, :]
    local_analysis = jnp.where(valid_cols, analysis_dep[0], jnp.zeros((), jnp.bfloat16))
    local_background = jnp.where(valid_cols, background_dep[0], jnp.zeros((), jnp.bfloat16))

    halves = local_analysis.reshape(width_block, PAIR, half)
    keep = jnp.where(pair_index == 0, halves[:, 0], halves[:, 1])
    give = jnp.where(pair_index == 0, halves[:, 1], halves[:, 0])
    got = swap_pair(give)
    pair_analysis = jnp.where(pair_index == 0, jnp.stack([keep, got]), jnp.stack([got, keep]))
    pair_analysis = pair_analysis.reshape(PAIR, width_block, chan_size, piece).transpose(2, 0, 1, 3)
    all_analysis = relay_gather(pair_analysis, quad_size)

    split_b = local_background.reshape(width_block, PAIR, chan_size, piece)
    by_loc = lax.all_to_all(split_b, "chan", 2, 0, tiled=True)
    by_loc = by_loc.reshape(quad_size, pair_rows, PAIR, piece).transpose(0, 2, 1, 3)
    by_loc = by_loc.reshape(quad_size * PAIR, pair_rows, piece)
    rows_here = lax.all_to_all(by_loc, ("tq", "th"), 0, 0, tiled=True)
    all_background = gather_chan(rows_here)

    rows_out = pair_rows // PAIR
    give_rows = lax.dynamic_slice_in_dim(all_background, (1 - pair_index) * rows_out, rows_out, axis=2)
    keep_rows = lax.dynamic_slice_in_dim(all_background, pair_index * rows_out, rows_out, axis=2)
    sent = swap_pair(lag_block(give_rows, all_analysis, cycle_total, max_lag, lag_total))
    summed = lag_block(keep_rows, all_analysis, cycle_total, max_lag, lag_total) + sent

    denominators = []
    for offset in range(max_lag + 1):
        span = cycle_total - offset
        denominators.append(
            jnp.sum(jnp.minimum(valid_counts[:span], valid_counts[offset:])).astype(jnp.float32)
        )
    divisor = jnp.stack([denominators[abs(k - max_lag)] for k in range(lag_total)])
    return summed / divisor[None, :, None]


def solution(mesh):
    tm_size, chan_size = mesh.devices.shape
    split = Mesh(mesh.devices.reshape(tm_size // PAIR, PAIR, chan_size), ("tq", "th", "chan"))
    in_specs = (P(("tq", "th"), "chan", None), P(("tq", "th"), "chan", None), P())
    out_specs = P(("tq", "th"), None, "chan")
    return jax.shard_map(body, mesh=split, in_specs=in_specs, out_specs=out_specs, check_vma=False)
```

```python
import jax
import jax.numpy as jnp
from jax import lax
from jax.sharding import Mesh, PartitionSpec as P

PAIR = 2


def swap_pair(x):
    return lax.ppermute(x, "th", [(0, 1), (1, 0)])


def gather_chan(x):
    size = lax.axis_size("chan")
    me = lax.axis_index("chan")
    bits = size.bit_length() - 1
    held = x[None]
    for bit in reversed(range(bits)):
        got = lax.ppermute(held, "chan", [(c, c ^ (1 << bit)) for c in range(size)])
        low = ((me >> bit) & 1) == 0
        first = jnp.where(low, held, got)
        second = jnp.where(low, got, held)
        held = jnp.concatenate([first, second], axis=0) if bit == bits - 1 else jnp.stack([first, second], axis=1).reshape((-1,) + x.shape)
    return held


def relay_gather(block, size):
    me = lax.axis_index("tq")
    from_left = from_right = block
    lefts, rights = [], []
    for _ in range(size - 1):
        from_left = lax.ppermute(from_left, "tq", [(i, i + 1) for i in range(size - 1)])
        from_right = lax.ppermute(from_right, "tq", [(i + 1, i) for i in range(size - 1)])
        lefts.append(from_left)
        rights.append(from_right)
    stacked = jnp.concatenate(lefts[::-1] + [block] + rights, axis=1)
    width = block.shape[1]
    return lax.dynamic_slice_in_dim(stacked, (size - 1 - me) * width, size * width, axis=1)


def contract(left, right):
    return lax.dot_general(
        left, right, (((0, 1, 3), (0, 1, 3)), ((), ())), preferred_element_type=jnp.float32
    )


def lag_block(background, analysis, cycle_total, max_lag, lag_total):
    pieces = [None] * lag_total
    for offset in range(max_lag + 1):
        span = cycle_total - offset
        pieces[max_lag + offset] = contract(background[:, offset:], analysis[:, :span])
        if offset > 0:
            pieces[max_lag - offset] = contract(background[:, :span], analysis[:, offset:])
    return jnp.stack(pieces, axis=1)


def body(analysis_dep, background_dep, valid_counts):
    cycle_total = valid_counts.shape[0]
    quad_size = lax.axis_size("tq")
    chan_size = lax.axis_size("chan")
    lag_total = 5
    max_lag = (lag_total - 1) // 2
    pair_index = lax.axis_index("th")
    cycle_index = lax.axis_index("tq") * PAIR + pair_index
    own_count = jnp.sum(
        jnp.where(jnp.arange(cycle_total, dtype=jnp.int32) == cycle_index, valid_counts, 0)
    )
    _, width_block, loc_total = analysis_dep.shape
    half = loc_total // PAIR
    piece = half // chan_size
    pair_rows = width_block * chan_size // quad_size
    valid_cols = (jnp.arange(loc_total, dtype=jnp.int32) < own_count)[None, :]
    local_analysis = jnp.where(valid_cols, analysis_dep[0], jnp.zeros((), jnp.bfloat16))
    local_background = jnp.where(valid_cols, background_dep[0], jnp.zeros((), jnp.bfloat16))

    halves = local_analysis.reshape(width_block, PAIR, half)
    keep = jnp.where(pair_index == 0, halves[:, 0], halves[:, 1])
    give = jnp.where(pair_index == 0, halves[:, 1], halves[:, 0])
    got = swap_pair(give)
    got, local_background = lax.optimization_barrier((got, local_background))
    pair_analysis = jnp.where(pair_index == 0, jnp.stack([keep, got]), jnp.stack([got, keep]))
    pair_analysis = pair_analysis.reshape(PAIR, width_block, chan_size, piece).transpose(2, 0, 1, 3)
    all_analysis = relay_gather(pair_analysis, quad_size)

    split_b = local_background.reshape(width_block, PAIR, chan_size, piece)
    by_loc = lax.all_to_all(split_b, "chan", 2, 0, tiled=True)
    by_loc = by_loc.reshape(quad_size, pair_rows, PAIR, piece).transpose(0, 2, 1, 3)
    by_loc = by_loc.reshape(quad_size * PAIR, pair_rows, piece)
    rows_here = lax.all_to_all(by_loc, ("tq", "th"), 0, 0, tiled=True)
    all_background = gather_chan(rows_here)

    rows_out = pair_rows // PAIR
    give_rows = lax.dynamic_slice_in_dim(all_background, (1 - pair_index) * rows_out, rows_out, axis=2)
    keep_rows = lax.dynamic_slice_in_dim(all_background, pair_index * rows_out, rows_out, axis=2)
    sent = swap_pair(lag_block(give_rows, all_analysis, cycle_total, max_lag, lag_total))
    summed = lag_block(keep_rows, all_analysis, cycle_total, max_lag, lag_total) + sent

    denominators = []
    for offset in range(max_lag + 1):
        span = cycle_total - offset
        denominators.append(
            jnp.sum(jnp.minimum(valid_counts[:span], valid_counts[offset:])).astype(jnp.float32)
        )
    divisor = jnp.stack([denominators[abs(k - max_lag)] for k in range(lag_total)])
    return summed / divisor[None, :, None]


def solution(mesh):
    tm_size, chan_size = mesh.devices.shape
    split = Mesh(mesh.devices.reshape(tm_size // PAIR, PAIR, chan_size), ("tq", "th", "chan"))
    in_specs = (P(("tq", "th"), "chan", None), P(("tq", "th"), "chan", None), P())
    out_specs = P(("tq", "th"), None, "chan")
    return jax.shard_map(body, mesh=split, in_specs=in_specs, out_specs=out_specs, check_vma=False)
```

```python
import jax
import jax.numpy as jnp
from jax import lax
from jax.sharding import Mesh, PartitionSpec as P

PAIR = 2


def swap_pair(x):
    return lax.ppermute(x, "th", [(0, 1), (1, 0)])


def gather_chan(x):
    size = lax.axis_size("chan")
    me = lax.axis_index("chan")
    bits = size.bit_length() - 1
    held = x[None]
    for bit in reversed(range(bits)):
        got = lax.ppermute(held, "chan", [(c, c ^ (1 << bit)) for c in range(size)])
        low = ((me >> bit) & 1) == 0
        first = jnp.where(low, held, got)
        second = jnp.where(low, got, held)
        held = jnp.concatenate([first, second], axis=0) if bit == bits - 1 else jnp.stack([first, second], axis=1).reshape((-1,) + x.shape)
    return held


def contract(left, right):
    return lax.dot_general(
        left, right, (((0, 1, 3), (0, 1, 3)), ((), ())), preferred_element_type=jnp.float32
    )


def lag_block(background, analysis, cycle_total, max_lag, lag_total):
    pieces = [None] * lag_total
    for offset in range(max_lag + 1):
        span = cycle_total - offset
        pieces[max_lag + offset] = contract(background[:, offset:], analysis[:, :span])
        if offset > 0:
            pieces[max_lag - offset] = contract(background[:, :span], analysis[:, offset:])
    return jnp.stack(pieces, axis=1)


def body(analysis_dep, background_dep, valid_counts):
    cycle_total = valid_counts.shape[0]
    quad_size = lax.axis_size("tq")
    chan_size = lax.axis_size("chan")
    lag_total = 5
    max_lag = (lag_total - 1) // 2
    pair_index = lax.axis_index("th")
    cycle_index = lax.axis_index("tq") * PAIR + pair_index
    own_count = jnp.sum(
        jnp.where(jnp.arange(cycle_total, dtype=jnp.int32) == cycle_index, valid_counts, 0)
    )
    _, width_block, loc_total = analysis_dep.shape
    half = loc_total // PAIR
    piece = half // chan_size
    pair_rows = width_block * chan_size // quad_size
    valid_cols = (jnp.arange(loc_total, dtype=jnp.int32) < own_count)[None, :]
    local_analysis = jnp.where(valid_cols, analysis_dep[0], jnp.zeros((), jnp.bfloat16))
    local_background = jnp.where(valid_cols, background_dep[0], jnp.zeros((), jnp.bfloat16))

    halves = local_analysis.reshape(width_block, PAIR, half)
    keep = jnp.where(pair_index == 0, halves[:, 0], halves[:, 1])
    give = jnp.where(pair_index == 0, halves[:, 1], halves[:, 0])
    got = swap_pair(give)
    pair_analysis = jnp.where(pair_index == 0, jnp.stack([keep, got]), jnp.stack([got, keep]))
    pair_analysis = pair_analysis.reshape(PAIR, width_block, chan_size, piece).transpose(2, 0, 1, 3)
    all_analysis = lax.all_gather(pair_analysis, "tq", axis=1, tiled=True)

    split_b = local_background.reshape(width_block, PAIR, chan_size, piece)
    by_loc = lax.all_to_all(split_b, "chan", 2, 0, tiled=True)
    by_loc = by_loc.reshape(quad_size, pair_rows, PAIR, piece).transpose(0, 2, 1, 3)
    by_loc = by_loc.reshape(quad_size * PAIR, pair_rows, piece)
    rows_here = lax.all_to_all(by_loc, ("tq", "th"), 0, 0, tiled=True)
    rows_out = pair_rows // PAIR
    swapped = jnp.concatenate([rows_here[:, rows_out:], rows_here[:, :rows_out]], axis=1)
    own_first = jnp.where(pair_index == 0, rows_here, swapped)
    all_background = gather_chan(own_first)

    keep_rows = all_background[:, :, :rows_out]
    give_rows = all_background[:, :, rows_out:]
    sent = swap_pair(lag_block(give_rows, all_analysis, cycle_total, max_lag, lag_total))
    summed = lag_block(keep_rows, all_analysis, cycle_total, max_lag, lag_total) + sent

    denominators = []
    for offset in range(max_lag + 1):
        span = cycle_total - offset
        denominators.append(
            jnp.sum(jnp.minimum(valid_counts[:span], valid_counts[offset:])).astype(jnp.float32)
        )
    divisor = jnp.stack([denominators[abs(k - max_lag)] for k in range(lag_total)])
    return summed / divisor[None, :, None]


def solution(mesh):
    tm_size, chan_size = mesh.devices.shape
    split = Mesh(mesh.devices.reshape(tm_size // PAIR, PAIR, chan_size), ("tq", "th", "chan"))
    in_specs = (P(("tq", "th"), "chan", None), P(("tq", "th"), "chan", None), P())
    out_specs = P(("tq", "th"), None, "chan")
    return jax.shard_map(body, mesh=split, in_specs=in_specs, out_specs=out_specs, check_vma=False)
```

```python
import jax
import jax.numpy as jnp
from jax import lax
from jax.sharding import Mesh, PartitionSpec as P

PAIR = 2


def swap_pair(x):
    return lax.ppermute(x, "th", [(0, 1), (1, 0)])


def gather_chan(x):
    size = lax.axis_size("chan")
    me = lax.axis_index("chan")
    bits = size.bit_length() - 1
    held = x[None]
    for bit in reversed(range(bits)):
        got = lax.ppermute(held, "chan", [(c, c ^ (1 << bit)) for c in range(size)])
        low = ((me >> bit) & 1) == 0
        first = jnp.where(low, held, got)
        second = jnp.where(low, got, held)
        held = jnp.concatenate([first, second], axis=0) if bit == bits - 1 else jnp.stack([first, second], axis=1).reshape((-1,) + x.shape)
    return held


def contract(left, right):
    return lax.dot_general(
        left, right, (((0, 1, 3), (0, 1, 3)), ((), ())), preferred_element_type=jnp.float32
    )


def lag_block(background, analysis, cycle_total, max_lag, lag_total):
    pieces = [None] * lag_total
    for offset in range(max_lag + 1):
        span = cycle_total - offset
        pieces[max_lag + offset] = contract(background[:, offset:], analysis[:, :span])
        if offset > 0:
            pieces[max_lag - offset] = contract(background[:, :span], analysis[:, offset:])
    return jnp.stack(pieces, axis=1)


def body(analysis_dep, background_dep, valid_counts):
    cycle_total = valid_counts.shape[0]
    quad_size = lax.axis_size("tq")
    chan_size = lax.axis_size("chan")
    lag_total = 5
    max_lag = (lag_total - 1) // 2
    pair_index = lax.axis_index("th")
    cycle_index = lax.axis_index("tq") * PAIR + pair_index
    own_count = jnp.sum(
        jnp.where(jnp.arange(cycle_total, dtype=jnp.int32) == cycle_index, valid_counts, 0)
    )
    _, width_block, loc_total = analysis_dep.shape
    half = loc_total // PAIR
    piece = half // chan_size
    pair_rows = width_block * chan_size // quad_size
    valid_cols = (jnp.arange(loc_total, dtype=jnp.int32) < own_count)[None, :]
    local_analysis = jnp.where(valid_cols, analysis_dep[0], jnp.zeros((), jnp.bfloat16))
    local_background = jnp.where(valid_cols, background_dep[0], jnp.zeros((), jnp.bfloat16))

    low_half = local_analysis[:, :half]
    high_half = local_analysis[:, half:]
    keep = jnp.where(pair_index == 0, low_half, high_half)
    give = jnp.where(pair_index == 0, high_half, low_half)
    got = swap_pair(give)
    pair_analysis = jnp.where(pair_index == 0, jnp.stack([keep, got]), jnp.stack([got, keep]))
    pair_analysis = pair_analysis.reshape(PAIR, width_block, chan_size, piece).transpose(2, 0, 1, 3)
    all_analysis = lax.all_gather(pair_analysis, "tq", axis=1, tiled=True)

    split_b = local_background.reshape(width_block, PAIR, chan_size, piece)
    by_loc = lax.all_to_all(split_b, "chan", 2, 0, tiled=True)
    by_loc = by_loc.reshape(quad_size, pair_rows, PAIR, piece).transpose(0, 2, 1, 3)
    by_loc = by_loc.reshape(quad_size * PAIR, pair_rows, piece)
    rows_here = lax.all_to_all(by_loc, ("tq", "th"), 0, 0, tiled=True)
    all_background = gather_chan(rows_here)

    rows_out = pair_rows // PAIR
    give_rows = lax.dynamic_slice_in_dim(all_background, (1 - pair_index) * rows_out, rows_out, axis=2)
    keep_rows = lax.dynamic_slice_in_dim(all_background, pair_index * rows_out, rows_out, axis=2)
    sent = swap_pair(lag_block(give_rows, all_analysis, cycle_total, max_lag, lag_total))
    summed = lag_block(keep_rows, all_analysis, cycle_total, max_lag, lag_total) + sent

    denominators = []
    for offset in range(max_lag + 1):
        span = cycle_total - offset
        denominators.append(
            jnp.sum(jnp.minimum(valid_counts[:span], valid_counts[offset:])).astype(jnp.float32)
        )
    divisor = jnp.stack([denominators[abs(k - max_lag)] for k in range(lag_total)])
    return summed / divisor[None, :, None]


def solution(mesh):
    tm_size, chan_size = mesh.devices.shape
    split = Mesh(mesh.devices.reshape(tm_size // PAIR, PAIR, chan_size), ("tq", "th", "chan"))
    in_specs = (P(("tq", "th"), "chan", None), P(("tq", "th"), "chan", None), P())
    out_specs = P(("tq", "th"), None, "chan")
    return jax.shard_map(body, mesh=split, in_specs=in_specs, out_specs=out_specs, check_vma=False)
```

```python
import jax
import jax.numpy as jnp
from jax import lax
from jax.sharding import Mesh, PartitionSpec as P

PAIR = 2


def swap_pair(x):
    return lax.ppermute(x, "th", [(0, 1), (1, 0)])


def gather_chan(x):
    size = lax.axis_size("chan")
    me = lax.axis_index("chan")
    bits = size.bit_length() - 1
    held = x[None]
    for bit in reversed(range(bits)):
        got = lax.ppermute(held, "chan", [(c, c ^ (1 << bit)) for c in range(size)])
        low = ((me >> bit) & 1) == 0
        first = jnp.where(low, held, got)
        second = jnp.where(low, got, held)
        held = jnp.concatenate([first, second], axis=0) if bit == bits - 1 else jnp.stack([first, second], axis=1).reshape((-1,) + x.shape)
    return held


def contract(left, right):
    return lax.dot_general(
        left, right, (((0, 1, 3), (0, 1, 3)), ((), ())), preferred_element_type=jnp.float32
    )


def lag_block(background, analysis, cycle_total, max_lag, lags):
    pieces = []
    for k in lags:
        offset = k - max_lag
        if offset >= 0:
            span = cycle_total - offset
            pieces.append(contract(background[:, offset:], analysis[:, :span]))
        else:
            span = cycle_total + offset
            pieces.append(contract(background[:, :span], analysis[:, -offset:]))
    return jnp.stack(pieces, axis=1)


def body(analysis_dep, background_dep, valid_counts):
    cycle_total = valid_counts.shape[0]
    quad_size = lax.axis_size("tq")
    chan_size = lax.axis_size("chan")
    lag_total = 5
    max_lag = (lag_total - 1) // 2
    pair_index = lax.axis_index("th")
    cycle_index = lax.axis_index("tq") * PAIR + pair_index
    own_count = jnp.sum(
        jnp.where(jnp.arange(cycle_total, dtype=jnp.int32) == cycle_index, valid_counts, 0)
    )
    _, width_block, loc_total = analysis_dep.shape
    half = loc_total // PAIR
    piece = half // chan_size
    pair_rows = width_block * chan_size // quad_size
    valid_cols = (jnp.arange(loc_total, dtype=jnp.int32) < own_count)[None, :]
    local_analysis = jnp.where(valid_cols, analysis_dep[0], jnp.zeros((), jnp.bfloat16))
    local_background = jnp.where(valid_cols, background_dep[0], jnp.zeros((), jnp.bfloat16))

    low_half = local_analysis[:, :half]
    high_half = local_analysis[:, half:]
    keep = jnp.where(pair_index == 0, low_half, high_half)
    give = jnp.where(pair_index == 0, high_half, low_half)
    got = swap_pair(give)
    pair_analysis = jnp.where(pair_index == 0, jnp.stack([keep, got]), jnp.stack([got, keep]))
    pair_analysis = pair_analysis.reshape(PAIR, width_block, chan_size, piece).transpose(2, 0, 1, 3)
    all_analysis = lax.all_gather(pair_analysis, "tq", axis=1, tiled=True)

    split_b = local_background.reshape(width_block, PAIR, chan_size, piece)
    by_loc = lax.all_to_all(split_b, "chan", 2, 0, tiled=True)
    by_loc = by_loc.reshape(quad_size, pair_rows, PAIR, piece).transpose(0, 2, 1, 3)
    by_loc = by_loc.reshape(quad_size * PAIR, pair_rows, piece)
    rows_here = lax.all_to_all(by_loc, ("tq", "th"), 0, 0, tiled=True)
    all_background = gather_chan(rows_here)

    rows_out = pair_rows // PAIR
    give_rows = lax.dynamic_slice_in_dim(all_background, (1 - pair_index) * rows_out, rows_out, axis=2)
    keep_rows = lax.dynamic_slice_in_dim(all_background, pair_index * rows_out, rows_out, axis=2)
    outer = (0, lag_total - 1)
    inner = tuple(range(1, lag_total - 1))
    sent_outer = swap_pair(lag_block(give_rows, all_analysis, cycle_total, max_lag, outer))
    sent_inner = swap_pair(lag_block(give_rows, all_analysis, cycle_total, max_lag, inner))
    own = lag_block(keep_rows, all_analysis, cycle_total, max_lag, range(lag_total))
    sent = jnp.concatenate([sent_outer[:, :1], sent_inner, sent_outer[:, 1:]], axis=1)
    summed = own + sent

    denominators = []
    for offset in range(max_lag + 1):
        span = cycle_total - offset
        denominators.append(
            jnp.sum(jnp.minimum(valid_counts[:span], valid_counts[offset:])).astype(jnp.float32)
        )
    divisor = jnp.stack([denominators[abs(k - max_lag)] for k in range(lag_total)])
    return summed / divisor[None, :, None]


def solution(mesh):
    tm_size, chan_size = mesh.devices.shape
    split = Mesh(mesh.devices.reshape(tm_size // PAIR, PAIR, chan_size), ("tq", "th", "chan"))
    in_specs = (P(("tq", "th"), "chan", None), P(("tq", "th"), "chan", None), P())
    out_specs = P(("tq", "th"), None, "chan")
    return jax.shard_map(body, mesh=split, in_specs=in_specs, out_specs=out_specs, check_vma=False)
```

```python
import jax
import jax.numpy as jnp
from jax import lax
from jax.sharding import Mesh, PartitionSpec as P

PAIR = 2


def swap_pair(x):
    return lax.ppermute(x, "th", [(0, 1), (1, 0)])


def gather_chan(x):
    size = lax.axis_size("chan")
    me = lax.axis_index("chan")
    bits = size.bit_length() - 1
    held = x[None]
    for bit in reversed(range(bits)):
        got = lax.ppermute(held, "chan", [(c, c ^ (1 << bit)) for c in range(size)])
        low = ((me >> bit) & 1) == 0
        held = jnp.concatenate([jnp.where(low, held, got), jnp.where(low, got, held)], axis=0)
    return held


def bit_reversed(x, axis, size):
    bits = size.bit_length() - 1
    shape = x.shape[:axis] + (2,) * bits + x.shape[axis + 1:]
    order = list(range(axis)) + [axis + bits - 1 - k for k in range(bits)] + list(range(axis + bits, len(shape)))
    return x.reshape(shape).transpose(order).reshape(x.shape)


def contract(left, right):
    return lax.dot_general(
        left, right, (((0, 1, 3), (0, 1, 3)), ((), ())), preferred_element_type=jnp.float32
    )


def lag_block(background, analysis, cycle_total, max_lag, lags):
    pieces = []
    for k in lags:
        offset = k - max_lag
        if offset >= 0:
            span = cycle_total - offset
            pieces.append(contract(background[:, offset:], analysis[:, :span]))
        else:
            span = cycle_total + offset
            pieces.append(contract(background[:, :span], analysis[:, -offset:]))
    return jnp.stack(pieces, axis=1)


def body(analysis_dep, background_dep, valid_counts):
    cycle_total = valid_counts.shape[0]
    quad_size = lax.axis_size("tq")
    chan_size = lax.axis_size("chan")
    lag_total = 5
    max_lag = (lag_total - 1) // 2
    pair_index = lax.axis_index("th")
    cycle_index = lax.axis_index("tq") * PAIR + pair_index
    own_count = jnp.sum(
        jnp.where(jnp.arange(cycle_total, dtype=jnp.int32) == cycle_index, valid_counts, 0)
    )
    _, width_block, loc_total = analysis_dep.shape
    half = loc_total // PAIR
    piece = half // chan_size
    pair_rows = width_block * chan_size // quad_size
    valid_cols = (jnp.arange(loc_total, dtype=jnp.int32) < own_count)[None, :]
    local_analysis = jnp.where(valid_cols, analysis_dep[0], jnp.zeros((), jnp.bfloat16))
    local_background = jnp.where(valid_cols, background_dep[0], jnp.zeros((), jnp.bfloat16))

    low_half = local_analysis[:, :half]
    high_half = local_analysis[:, half:]
    keep = jnp.where(pair_index == 0, low_half, high_half)
    give = jnp.where(pair_index == 0, high_half, low_half)
    got = swap_pair(give)
    pair_analysis = jnp.where(pair_index == 0, jnp.stack([keep, got]), jnp.stack([got, keep]))
    pair_analysis = pair_analysis.reshape(PAIR, width_block, chan_size, piece).transpose(2, 0, 1, 3)
    pair_analysis = bit_reversed(pair_analysis, 0, chan_size)
    all_analysis = lax.all_gather(pair_analysis, "tq", axis=1, tiled=True)

    split_b = local_background.reshape(width_block, PAIR, chan_size, piece)
    by_loc = lax.all_to_all(split_b, "chan", 2, 0, tiled=True)
    by_loc = by_loc.reshape(quad_size, pair_rows, PAIR, piece).transpose(0, 2, 1, 3)
    by_loc = by_loc.reshape(quad_size * PAIR, pair_rows, piece)
    rows_here = lax.all_to_all(by_loc, ("tq", "th"), 0, 0, tiled=True)
    all_background = gather_chan(rows_here)

    rows_out = pair_rows // PAIR
    give_rows = lax.dynamic_slice_in_dim(all_background, (1 - pair_index) * rows_out, rows_out, axis=2)
    keep_rows = lax.dynamic_slice_in_dim(all_background, pair_index * rows_out, rows_out, axis=2)
    outer = (0, lag_total - 1)
    inner = tuple(range(1, lag_total - 1))
    sent_outer = swap_pair(lag_block(give_rows, all_analysis, cycle_total, max_lag, outer))
    sent_inner = swap_pair(lag_block(give_rows, all_analysis, cycle_total, max_lag, inner))
    own = lag_block(keep_rows, all_analysis, cycle_total, max_lag, range(lag_total))
    sent = jnp.concatenate([sent_outer[:, :1], sent_inner, sent_outer[:, 1:]], axis=1)
    summed = own + sent

    denominators = []
    for offset in range(max_lag + 1):
        span = cycle_total - offset
        denominators.append(
            jnp.sum(jnp.minimum(valid_counts[:span], valid_counts[offset:])).astype(jnp.float32)
        )
    divisor = jnp.stack([denominators[abs(k - max_lag)] for k in range(lag_total)])
    return summed / divisor[None, :, None]


def solution(mesh):
    tm_size, chan_size = mesh.devices.shape
    split = Mesh(mesh.devices.reshape(tm_size // PAIR, PAIR, chan_size), ("tq", "th", "chan"))
    in_specs = (P(("tq", "th"), "chan", None), P(("tq", "th"), "chan", None), P())
    out_specs = P(("tq", "th"), None, "chan")
    return jax.shard_map(body, mesh=split, in_specs=in_specs, out_specs=out_specs, check_vma=False)
```

```python
import jax
import jax.numpy as jnp
from jax import lax
from jax.sharding import Mesh, PartitionSpec as P

PAIR = 2


def swap_pair(x):
    return lax.ppermute(x, "th", [(0, 1), (1, 0)])


def gather_chan(x):
    size = lax.axis_size("chan")
    me = lax.axis_index("chan")
    bits = size.bit_length() - 1
    held = x[None]
    for bit in reversed(range(bits)):
        got = lax.ppermute(held, "chan", [(c, c ^ (1 << bit)) for c in range(size)])
        low = ((me >> bit) & 1) == 0
        held = jnp.concatenate([jnp.where(low, held, got), jnp.where(low, got, held)], axis=0)
    return held


def bit_reversed(x, axis, size):
    bits = size.bit_length() - 1
    shape = x.shape[:axis] + (2,) * bits + x.shape[axis + 1:]
    order = list(range(axis)) + [axis + bits - 1 - k for k in range(bits)] + list(range(axis + bits, len(shape)))
    return x.reshape(shape).transpose(order).reshape(x.shape)


def contract(left, right):
    return lax.dot_general(
        left, right, (((0, 1, 3), (0, 1, 3)), ((), ())), preferred_element_type=jnp.float32
    )


def lag_block(background, analysis, cycle_total, max_lag, lags):
    pieces = []
    for k in lags:
        offset = k - max_lag
        if offset >= 0:
            span = cycle_total - offset
            pieces.append(contract(background[:, offset:], analysis[:, :span]))
        else:
            span = cycle_total + offset
            pieces.append(contract(background[:, :span], analysis[:, -offset:]))
    return jnp.stack(pieces, axis=1)


def body(analysis_dep, background_dep, valid_counts):
    cycle_total = valid_counts.shape[0]
    quad_size = lax.axis_size("tq")
    chan_size = lax.axis_size("chan")
    lag_total = 5
    max_lag = (lag_total - 1) // 2
    pair_index = lax.axis_index("th")
    cycle_index = lax.axis_index("tq") * PAIR + pair_index
    own_count = jnp.sum(
        jnp.where(jnp.arange(cycle_total, dtype=jnp.int32) == cycle_index, valid_counts, 0)
    )
    _, width_block, loc_total = analysis_dep.shape
    half = loc_total // PAIR
    piece = half // chan_size
    pair_rows = width_block * chan_size // quad_size
    valid_cols = (jnp.arange(loc_total, dtype=jnp.int32) < own_count)[None, :]
    local_analysis = jnp.where(valid_cols, analysis_dep[0], jnp.zeros((), jnp.bfloat16))
    local_background = jnp.where(valid_cols, background_dep[0], jnp.zeros((), jnp.bfloat16))

    low_half = local_analysis[:, :half]
    high_half = local_analysis[:, half:]
    keep = jnp.where(pair_index == 0, low_half, high_half)
    give = jnp.where(pair_index == 0, high_half, low_half)
    def by_piece(x):
        pieces_first = x.reshape(width_block, chan_size, piece).transpose(1, 0, 2)
        return bit_reversed(pieces_first, 0, chan_size)[:, None]

    same_parity = lax.all_gather(by_piece(keep), "tq", axis=1, tiled=True)
    got = swap_pair(give)
    other_parity = lax.all_gather(by_piece(got), "tq", axis=1, tiled=True)
    in_order = jnp.stack([same_parity, other_parity], axis=2)
    swapped = jnp.stack([other_parity, same_parity], axis=2)
    all_analysis = jnp.where(pair_index == 0, in_order, swapped)
    all_analysis = all_analysis.reshape(chan_size, cycle_total, width_block, piece)

    split_b = local_background.reshape(width_block, PAIR, chan_size, piece)
    by_loc = lax.all_to_all(split_b, "chan", 2, 0, tiled=True)
    by_loc = by_loc.reshape(quad_size, pair_rows, PAIR, piece).transpose(0, 2, 1, 3)
    by_loc = by_loc.reshape(quad_size * PAIR, pair_rows, piece)
    rows_here = lax.all_to_all(by_loc, ("tq", "th"), 0, 0, tiled=True)
    all_background = gather_chan(rows_here)

    rows_out = pair_rows // PAIR
    give_rows = lax.dynamic_slice_in_dim(all_background, (1 - pair_index) * rows_out, rows_out, axis=2)
    keep_rows = lax.dynamic_slice_in_dim(all_background, pair_index * rows_out, rows_out, axis=2)
    outer = (0, lag_total - 1)
    inner = tuple(range(1, lag_total - 1))
    sent_outer = swap_pair(lag_block(give_rows, all_analysis, cycle_total, max_lag, outer))
    sent_inner = swap_pair(lag_block(give_rows, all_analysis, cycle_total, max_lag, inner))
    own = lag_block(keep_rows, all_analysis, cycle_total, max_lag, range(lag_total))
    sent = jnp.concatenate([sent_outer[:, :1], sent_inner, sent_outer[:, 1:]], axis=1)
    summed = own + sent

    denominators = []
    for offset in range(max_lag + 1):
        span = cycle_total - offset
        denominators.append(
            jnp.sum(jnp.minimum(valid_counts[:span], valid_counts[offset:])).astype(jnp.float32)
        )
    divisor = jnp.stack([denominators[abs(k - max_lag)] for k in range(lag_total)])
    return summed / divisor[None, :, None]


def solution(mesh):
    tm_size, chan_size = mesh.devices.shape
    split = Mesh(mesh.devices.reshape(tm_size // PAIR, PAIR, chan_size), ("tq", "th", "chan"))
    in_specs = (P(("tq", "th"), "chan", None), P(("tq", "th"), "chan", None), P())
    out_specs = P(("tq", "th"), None, "chan")
    return jax.shard_map(body, mesh=split, in_specs=in_specs, out_specs=out_specs, check_vma=False)
```

```python
import jax
import jax.numpy as jnp
from jax import lax
from jax.sharding import Mesh, PartitionSpec as P

PAIR = 2


def swap_pair(x):
    return lax.ppermute(x, "th", [(0, 1), (1, 0)])


def gather_chan(x):
    size = lax.axis_size("chan")
    me = lax.axis_index("chan")
    bits = size.bit_length() - 1
    held = x[None]
    for bit in reversed(range(bits)):
        got = lax.ppermute(held, "chan", [(c, c ^ (1 << bit)) for c in range(size)])
        low = ((me >> bit) & 1) == 0
        held = jnp.concatenate([jnp.where(low, held, got), jnp.where(low, got, held)], axis=0)
    return held


def bit_reversed(x, axis, size):
    bits = size.bit_length() - 1
    shape = x.shape[:axis] + (2,) * bits + x.shape[axis + 1:]
    order = list(range(axis)) + [axis + bits - 1 - k for k in range(bits)] + list(range(axis + bits, len(shape)))
    return x.reshape(shape).transpose(order).reshape(x.shape)


def contract(left, right):
    return lax.dot_general(
        left, right, (((0, 1, 3), (0, 1, 3)), ((), ())), preferred_element_type=jnp.float32
    )


def lag_block(background, analysis, cycle_total, max_lag, lags):
    pieces = []
    for k in lags:
        offset = k - max_lag
        if offset >= 0:
            span = cycle_total - offset
            pieces.append(contract(background[:, offset:], analysis[:, :span]))
        else:
            span = cycle_total + offset
            pieces.append(contract(background[:, :span], analysis[:, -offset:]))
    return jnp.stack(pieces, axis=1)


def body(analysis_dep, background_dep, valid_counts):
    cycle_total = valid_counts.shape[0]
    quad_size = lax.axis_size("tq")
    chan_size = lax.axis_size("chan")
    lag_total = 5
    max_lag = (lag_total - 1) // 2
    pair_index = lax.axis_index("th")
    cycle_index = lax.axis_index("tq") * PAIR + pair_index
    own_count = jnp.sum(
        jnp.where(jnp.arange(cycle_total, dtype=jnp.int32) == cycle_index, valid_counts, 0)
    )
    _, width_block, loc_total = analysis_dep.shape
    half = loc_total // PAIR
    piece = half // chan_size
    pair_rows = width_block * chan_size // quad_size
    valid_cols = (jnp.arange(loc_total, dtype=jnp.int32) < own_count)[None, :]
    local_analysis = jnp.where(valid_cols, analysis_dep[0], jnp.zeros((), jnp.bfloat16))
    local_background = jnp.where(valid_cols, background_dep[0], jnp.zeros((), jnp.bfloat16))

    low_half = local_analysis[:, :half]
    high_half = local_analysis[:, half:]
    keep = jnp.where(pair_index == 0, low_half, high_half)
    give = jnp.where(pair_index == 0, high_half, low_half)
    def by_piece(x):
        pieces_first = x.reshape(width_block, chan_size, piece).transpose(1, 0, 2)
        return bit_reversed(pieces_first, 0, chan_size)[:, None]

    same_parity = lax.all_gather(by_piece(keep), "tq", axis=1, tiled=True)
    got = swap_pair(give)
    other_parity = lax.all_gather(by_piece(got), "tq", axis=1, tiled=True)
    slots = jnp.zeros(same_parity.shape[:2] + (PAIR,) + same_parity.shape[2:], jnp.bfloat16)
    slots = lax.dynamic_update_slice_in_dim(slots, same_parity[:, :, None], pair_index, axis=2)
    slots = lax.dynamic_update_slice_in_dim(slots, other_parity[:, :, None], 1 - pair_index, axis=2)
    all_analysis = slots.reshape(chan_size, cycle_total, width_block, piece)

    split_b = local_background.reshape(width_block, PAIR, chan_size, piece)
    by_loc = lax.all_to_all(split_b, "chan", 2, 0, tiled=True)
    by_loc = by_loc.reshape(quad_size, pair_rows, PAIR, piece).transpose(0, 2, 1, 3)
    by_loc = by_loc.reshape(quad_size * PAIR, pair_rows, piece)
    rows_here = lax.all_to_all(by_loc, ("tq", "th"), 0, 0, tiled=True)
    all_background = gather_chan(rows_here)

    rows_out = pair_rows // PAIR
    give_rows = lax.dynamic_slice_in_dim(all_background, (1 - pair_index) * rows_out, rows_out, axis=2)
    keep_rows = lax.dynamic_slice_in_dim(all_background, pair_index * rows_out, rows_out, axis=2)
    outer = (0, lag_total - 1)
    inner = tuple(range(1, lag_total - 1))
    sent_outer = swap_pair(lag_block(give_rows, all_analysis, cycle_total, max_lag, outer))
    sent_inner = swap_pair(lag_block(give_rows, all_analysis, cycle_total, max_lag, inner))
    own = lag_block(keep_rows, all_analysis, cycle_total, max_lag, range(lag_total))
    sent = jnp.concatenate([sent_outer[:, :1], sent_inner, sent_outer[:, 1:]], axis=1)
    summed = own + sent

    denominators = []
    for offset in range(max_lag + 1):
        span = cycle_total - offset
        denominators.append(
            jnp.sum(jnp.minimum(valid_counts[:span], valid_counts[offset:])).astype(jnp.float32)
        )
    divisor = jnp.stack([denominators[abs(k - max_lag)] for k in range(lag_total)])
    return summed / divisor[None, :, None]


def solution(mesh):
    tm_size, chan_size = mesh.devices.shape
    split = Mesh(mesh.devices.reshape(tm_size // PAIR, PAIR, chan_size), ("tq", "th", "chan"))
    in_specs = (P(("tq", "th"), "chan", None), P(("tq", "th"), "chan", None), P())
    out_specs = P(("tq", "th"), None, "chan")
    return jax.shard_map(body, mesh=split, in_specs=in_specs, out_specs=out_specs, check_vma=False)
```

```python
import jax
import jax.numpy as jnp
from jax import lax
from jax.sharding import Mesh, PartitionSpec as P

PAIR = 2


def swap_pair(x):
    return lax.ppermute(x, "th", [(0, 1), (1, 0)])


def gather_chan(x):
    size = lax.axis_size("chan")
    me = lax.axis_index("chan")
    bits = size.bit_length() - 1
    held = x[None]
    for bit in reversed(range(bits)):
        got = lax.ppermute(held, "chan", [(c, c ^ (1 << bit)) for c in range(size)])
        low = ((me >> bit) & 1) == 0
        held = jnp.concatenate([jnp.where(low, held, got), jnp.where(low, got, held)], axis=0)
    return held


def bit_reversed(x, axis, size):
    bits = size.bit_length() - 1
    shape = x.shape[:axis] + (2,) * bits + x.shape[axis + 1:]
    order = list(range(axis)) + [axis + bits - 1 - k for k in range(bits)] + list(range(axis + bits, len(shape)))
    return x.reshape(shape).transpose(order).reshape(x.shape)


def contract(left, right):
    return lax.dot_general(
        left, right, (((0, 1, 3), (0, 1, 3)), ((), ())), preferred_element_type=jnp.float32
    )


def lag_block(background, analysis, cycle_total, max_lag, lags):
    pieces = []
    for k in lags:
        offset = k - max_lag
        if offset >= 0:
            span = cycle_total - offset
            pieces.append(contract(background[:, offset:], analysis[:, :span]))
        else:
            span = cycle_total + offset
            pieces.append(contract(background[:, :span], analysis[:, -offset:]))
    return jnp.stack(pieces, axis=1)


def body(analysis_dep, background_dep, valid_counts):
    cycle_total = valid_counts.shape[0]
    quad_size = lax.axis_size("tq")
    chan_size = lax.axis_size("chan")
    lag_total = 5
    max_lag = (lag_total - 1) // 2
    pair_index = lax.axis_index("th")
    cycle_index = lax.axis_index("tq") * PAIR + pair_index
    own_count = jnp.sum(
        jnp.where(jnp.arange(cycle_total, dtype=jnp.int32) == cycle_index, valid_counts, 0)
    )
    _, width_block, loc_total = analysis_dep.shape
    half = loc_total // PAIR
    piece = half // chan_size
    pair_rows = width_block * chan_size // quad_size
    valid_cols = (jnp.arange(loc_total, dtype=jnp.int32) < own_count)[None, :]
    local_analysis = jnp.where(valid_cols, analysis_dep[0], jnp.zeros((), jnp.bfloat16))
    local_background = jnp.where(valid_cols, background_dep[0], jnp.zeros((), jnp.bfloat16))

    low_half = local_analysis[:, :half]
    high_half = local_analysis[:, half:]
    keep = jnp.where(pair_index == 0, low_half, high_half)
    give = jnp.where(pair_index == 0, high_half, low_half)
    def by_piece(x):
        pieces_first = x.reshape(width_block, chan_size, piece).transpose(1, 0, 2)
        return bit_reversed(pieces_first, 0, chan_size)[:, None]

    same_parity = lax.all_gather(by_piece(keep), "tq", axis=1, tiled=True)
    got = swap_pair(give)
    other_parity = lax.all_gather(by_piece(got), "tq", axis=1, tiled=True)
    in_order = jnp.stack([same_parity, other_parity], axis=2)
    swapped = jnp.stack([other_parity, same_parity], axis=2)
    all_analysis = jnp.where(pair_index == 0, in_order, swapped)
    all_analysis = all_analysis.reshape(chan_size, cycle_total, width_block, piece)

    split_b = local_background.reshape(width_block, PAIR, chan_size, piece)
    by_loc = lax.all_to_all(split_b, "chan", 2, 0, tiled=True)
    by_loc = by_loc.reshape(quad_size, pair_rows, PAIR, piece).transpose(0, 2, 1, 3)
    by_loc = by_loc.reshape(quad_size * PAIR, pair_rows, piece)
    rows_here = lax.all_to_all(by_loc, ("tq", "th"), 0, 0, tiled=True)
    all_background = gather_chan(rows_here)

    rows_out = pair_rows // PAIR
    give_rows = lax.dynamic_slice_in_dim(all_background, (1 - pair_index) * rows_out, rows_out, axis=2)
    keep_rows = lax.dynamic_slice_in_dim(all_background, pair_index * rows_out, rows_out, axis=2)
    outer = (0, lag_total - 1)
    inner = tuple(range(1, lag_total - 1))
    def parity_cycles(x, parity):
        return jnp.where(parity == 0, x[:, 0::PAIR], x[:, 1::PAIR])

    give_same = parity_cycles(give_rows, pair_index)
    give_other = parity_cycles(give_rows, 1 - pair_index)
    shift = max_lag // PAIR
    outer_parts = []
    for k in outer:
        if k < max_lag:
            left, right = slice(None, quad_size - shift), slice(shift, None)
        else:
            left, right = slice(shift, None), slice(None, quad_size - shift)
        outer_parts.append(
            contract(give_same[:, left], same_parity[:, right])
            + contract(give_other[:, left], other_parity[:, right])
        )
    sent_outer = swap_pair(jnp.stack(outer_parts, axis=1))
    sent_inner = swap_pair(lag_block(give_rows, all_analysis, cycle_total, max_lag, inner))
    own = lag_block(keep_rows, all_analysis, cycle_total, max_lag, range(lag_total))
    sent = jnp.concatenate([sent_outer[:, :1], sent_inner, sent_outer[:, 1:]], axis=1)
    summed = own + sent

    denominators = []
    for offset in range(max_lag + 1):
        span = cycle_total - offset
        denominators.append(
            jnp.sum(jnp.minimum(valid_counts[:span], valid_counts[offset:])).astype(jnp.float32)
        )
    divisor = jnp.stack([denominators[abs(k - max_lag)] for k in range(lag_total)])
    return summed / divisor[None, :, None]


def solution(mesh):
    tm_size, chan_size = mesh.devices.shape
    split = Mesh(mesh.devices.reshape(tm_size // PAIR, PAIR, chan_size), ("tq", "th", "chan"))
    in_specs = (P(("tq", "th"), "chan", None), P(("tq", "th"), "chan", None), P())
    out_specs = P(("tq", "th"), None, "chan")
    return jax.shard_map(body, mesh=split, in_specs=in_specs, out_specs=out_specs, check_vma=False)
```

```python
import jax
import jax.numpy as jnp
from jax import lax
from jax.sharding import Mesh, PartitionSpec as P

PAIR = 2


def swap_pair(x):
    return lax.ppermute(x, "th", [(0, 1), (1, 0)])


def gather_chan(x):
    size = lax.axis_size("chan")
    me = lax.axis_index("chan")
    bits = size.bit_length() - 1
    held = x[None]
    for bit in reversed(range(bits)):
        got = lax.ppermute(held, "chan", [(c, c ^ (1 << bit)) for c in range(size)])
        low = ((me >> bit) & 1) == 0
        held = jnp.concatenate([jnp.where(low, held, got), jnp.where(low, got, held)], axis=0)
    return held


def bit_reversed(x, axis, size):
    bits = size.bit_length() - 1
    shape = x.shape[:axis] + (2,) * bits + x.shape[axis + 1:]
    order = list(range(axis)) + [axis + bits - 1 - k for k in range(bits)] + list(range(axis + bits, len(shape)))
    return x.reshape(shape).transpose(order).reshape(x.shape)


def contract(left, right):
    return lax.dot_general(
        left, right, (((0, 1, 3), (0, 1, 3)), ((), ())), preferred_element_type=jnp.float32
    )


def lag_block(background, analysis, cycle_total, max_lag, lags):
    pieces = []
    for k in lags:
        offset = k - max_lag
        if offset >= 0:
            span = cycle_total - offset
            pieces.append(contract(background[:, offset:], analysis[:, :span]))
        else:
            span = cycle_total + offset
            pieces.append(contract(background[:, :span], analysis[:, -offset:]))
    return jnp.stack(pieces, axis=1)


def body(analysis_dep, background_dep, valid_counts):
    cycle_total = valid_counts.shape[0]
    quad_size = lax.axis_size("tq")
    chan_size = lax.axis_size("chan")
    lag_total = 5
    max_lag = (lag_total - 1) // 2
    pair_index = lax.axis_index("th")
    cycle_index = lax.axis_index("tq") * PAIR + pair_index
    own_count = jnp.sum(
        jnp.where(jnp.arange(cycle_total, dtype=jnp.int32) == cycle_index, valid_counts, 0)
    )
    _, width_block, loc_total = analysis_dep.shape
    half = loc_total // PAIR
    piece = half // chan_size
    pair_rows = width_block * chan_size // quad_size
    valid_cols = (jnp.arange(loc_total, dtype=jnp.int32) < own_count)[None, :]
    local_analysis = jnp.where(valid_cols, analysis_dep[0], jnp.zeros((), jnp.bfloat16))
    local_background = jnp.where(valid_cols, background_dep[0], jnp.zeros((), jnp.bfloat16))

    low_half = local_analysis[:, :half]
    high_half = local_analysis[:, half:]
    keep = jnp.where(pair_index == 0, low_half, high_half)
    give = jnp.where(pair_index == 0, high_half, low_half)
    def by_piece(x):
        pieces_first = x.reshape(width_block, chan_size, piece).transpose(1, 0, 2)
        return bit_reversed(pieces_first, 0, chan_size)[:, None]

    same_parity = lax.all_gather(by_piece(keep), "tq", axis=1, tiled=True)
    got = swap_pair(give)
    other_parity = lax.all_gather(by_piece(got), "tq", axis=1, tiled=True)
    split_b = local_background.reshape(width_block, PAIR, chan_size, piece)
    by_loc = lax.all_to_all(split_b, "chan", 2, 0, tiled=True)
    by_loc = by_loc.reshape(quad_size, pair_rows, PAIR, piece).transpose(0, 2, 1, 3)
    by_loc = by_loc.reshape(quad_size * PAIR, pair_rows, piece)
    rows_here = lax.all_to_all(by_loc, ("tq", "th"), 0, 0, tiled=True)
    all_background = gather_chan(rows_here)

    rows_out = pair_rows // PAIR
    give_rows = lax.dynamic_slice_in_dim(all_background, (1 - pair_index) * rows_out, rows_out, axis=2)
    keep_rows = lax.dynamic_slice_in_dim(all_background, pair_index * rows_out, rows_out, axis=2)
    outer = (0, lag_total - 1)
    inner = tuple(range(1, lag_total - 1))
    def parity_cycles(x, parity):
        return jnp.where(parity == 0, x[:, 0::PAIR], x[:, 1::PAIR])

    give_same = parity_cycles(give_rows, pair_index)
    give_other = parity_cycles(give_rows, 1 - pair_index)
    shift = max_lag // PAIR
    outer_parts = []
    for k in outer:
        if k < max_lag:
            left, right = slice(None, quad_size - shift), slice(shift, None)
        else:
            left, right = slice(shift, None), slice(None, quad_size - shift)
        outer_parts.append(
            contract(give_same[:, left], same_parity[:, right])
            + contract(give_other[:, left], other_parity[:, right])
        )
    outer_partial, same_late, other_late = lax.optimization_barrier(
        (jnp.stack(outer_parts, axis=1), same_parity, other_parity)
    )
    sent_outer = swap_pair(outer_partial)
    in_order = jnp.stack([same_late, other_late], axis=2)
    swapped = jnp.stack([other_late, same_late], axis=2)
    all_analysis = jnp.where(pair_index == 0, in_order, swapped)
    all_analysis = all_analysis.reshape(chan_size, cycle_total, width_block, piece)
    sent_inner = swap_pair(lag_block(give_rows, all_analysis, cycle_total, max_lag, inner))
    own = lag_block(keep_rows, all_analysis, cycle_total, max_lag, range(lag_total))
    sent = jnp.concatenate([sent_outer[:, :1], sent_inner, sent_outer[:, 1:]], axis=1)
    summed = own + sent

    denominators = []
    for offset in range(max_lag + 1):
        span = cycle_total - offset
        denominators.append(
            jnp.sum(jnp.minimum(valid_counts[:span], valid_counts[offset:])).astype(jnp.float32)
        )
    divisor = jnp.stack([denominators[abs(k - max_lag)] for k in range(lag_total)])
    return summed / divisor[None, :, None]


def solution(mesh):
    tm_size, chan_size = mesh.devices.shape
    split = Mesh(mesh.devices.reshape(tm_size // PAIR, PAIR, chan_size), ("tq", "th", "chan"))
    in_specs = (P(("tq", "th"), "chan", None), P(("tq", "th"), "chan", None), P())
    out_specs = P(("tq", "th"), None, "chan")
    return jax.shard_map(body, mesh=split, in_specs=in_specs, out_specs=out_specs, check_vma=False)
```

```python
import jax
import jax.numpy as jnp
from jax import lax
from jax.sharding import Mesh, PartitionSpec as P

PAIR = 2


def swap_pair(x):
    return lax.ppermute(x, "th", [(0, 1), (1, 0)])


def gather_chan(x):
    size = lax.axis_size("chan")
    me = lax.axis_index("chan")
    bits = size.bit_length() - 1
    held = x[None]
    for bit in reversed(range(bits)):
        got = lax.ppermute(held, "chan", [(c, c ^ (1 << bit)) for c in range(size)])
        low = ((me >> bit) & 1) == 0
        held = jnp.concatenate([jnp.where(low, held, got), jnp.where(low, got, held)], axis=0)
    return held


def bit_reversed(x, axis, size):
    bits = size.bit_length() - 1
    shape = x.shape[:axis] + (2,) * bits + x.shape[axis + 1:]
    order = list(range(axis)) + [axis + bits - 1 - k for k in range(bits)] + list(range(axis + bits, len(shape)))
    return x.reshape(shape).transpose(order).reshape(x.shape)


def contract(left, right):
    return lax.dot_general(
        left, right, (((0, 1, 3), (0, 1, 3)), ((), ())), preferred_element_type=jnp.float32
    )


def lag_block(background, analysis, cycle_total, max_lag, lags):
    pieces = []
    for k in lags:
        offset = k - max_lag
        if offset >= 0:
            span = cycle_total - offset
            pieces.append(contract(background[:, offset:], analysis[:, :span]))
        else:
            span = cycle_total + offset
            pieces.append(contract(background[:, :span], analysis[:, -offset:]))
    return jnp.stack(pieces, axis=1)


def body(analysis_dep, background_dep, valid_counts):
    cycle_total = valid_counts.shape[0]
    quad_size = lax.axis_size("tq")
    chan_size = lax.axis_size("chan")
    lag_total = 5
    max_lag = (lag_total - 1) // 2
    pair_index = lax.axis_index("th")
    cycle_index = lax.axis_index("tq") * PAIR + pair_index
    own_count = jnp.sum(
        jnp.where(jnp.arange(cycle_total, dtype=jnp.int32) == cycle_index, valid_counts, 0)
    )
    _, width_block, loc_total = analysis_dep.shape
    half = loc_total // PAIR
    piece = half // chan_size
    pair_rows = width_block * chan_size // quad_size
    valid_cols = (jnp.arange(loc_total, dtype=jnp.int32) < own_count)[None, :]
    local_analysis = jnp.where(valid_cols, analysis_dep[0], jnp.zeros((), jnp.bfloat16))
    local_background = jnp.where(valid_cols, background_dep[0], jnp.zeros((), jnp.bfloat16))

    low_half = local_analysis[:, :half]
    high_half = local_analysis[:, half:]
    keep = jnp.where(pair_index == 0, low_half, high_half)
    give = jnp.where(pair_index == 0, high_half, low_half)
    def by_piece(x):
        pieces_first = x.reshape(width_block, chan_size, piece).transpose(1, 0, 2)
        return bit_reversed(pieces_first, 0, chan_size)[:, None]

    same_parity = lax.all_gather(by_piece(keep), "tq", axis=1, tiled=True)
    got = swap_pair(give)
    other_parity = lax.all_gather(by_piece(got), "tq", axis=1, tiled=True)
    in_order = jnp.stack([same_parity, other_parity], axis=2)
    swapped = jnp.stack([other_parity, same_parity], axis=2)
    all_analysis = jnp.where(pair_index == 0, in_order, swapped)
    all_analysis = all_analysis.reshape(chan_size, cycle_total, width_block, piece)

    split_b = local_background.reshape(width_block, PAIR, chan_size, piece)
    by_loc = lax.all_to_all(split_b, "chan", 2, 0, tiled=True)
    by_loc = by_loc.reshape(quad_size, pair_rows, PAIR, piece).transpose(0, 2, 1, 3)
    by_loc = by_loc.reshape(quad_size * PAIR, pair_rows, piece)
    rows_here = lax.all_to_all(by_loc, ("tq", "th"), 0, 0, tiled=True)
    all_background = gather_chan(rows_here)

    rows_out = pair_rows // PAIR
    give_rows = lax.dynamic_slice_in_dim(all_background, (1 - pair_index) * rows_out, rows_out, axis=2)
    keep_rows = lax.dynamic_slice_in_dim(all_background, pair_index * rows_out, rows_out, axis=2)
    first = (0,)
    second = (lag_total - 1,)
    inner = tuple(range(1, lag_total - 1))
    sent_first = swap_pair(lag_block(give_rows, all_analysis, cycle_total, max_lag, first))
    sent_second = swap_pair(lag_block(give_rows, all_analysis, cycle_total, max_lag, second))
    sent_inner = swap_pair(lag_block(give_rows, all_analysis, cycle_total, max_lag, inner))
    own = lag_block(keep_rows, all_analysis, cycle_total, max_lag, range(lag_total))
    sent = jnp.concatenate([sent_first, sent_inner, sent_second], axis=1)
    summed = own + sent

    denominators = []
    for offset in range(max_lag + 1):
        span = cycle_total - offset
        denominators.append(
            jnp.sum(jnp.minimum(valid_counts[:span], valid_counts[offset:])).astype(jnp.float32)
        )
    divisor = jnp.stack([denominators[abs(k - max_lag)] for k in range(lag_total)])
    return summed / divisor[None, :, None]


def solution(mesh):
    tm_size, chan_size = mesh.devices.shape
    split = Mesh(mesh.devices.reshape(tm_size // PAIR, PAIR, chan_size), ("tq", "th", "chan"))
    in_specs = (P(("tq", "th"), "chan", None), P(("tq", "th"), "chan", None), P())
    out_specs = P(("tq", "th"), None, "chan")
    return jax.shard_map(body, mesh=split, in_specs=in_specs, out_specs=out_specs, check_vma=False)
```

```python
import jax
import jax.numpy as jnp
from jax import lax
from jax.sharding import Mesh, PartitionSpec as P

PAIR = 2


def swap_pair(x):
    return lax.ppermute(x, "th", [(0, 1), (1, 0)])


def gather_chan(x):
    size = lax.axis_size("chan")
    me = lax.axis_index("chan")
    bits = size.bit_length() - 1
    held = x[None]
    for bit in reversed(range(bits)):
        got = lax.ppermute(held, "chan", [(c, c ^ (1 << bit)) for c in range(size)])
        low = ((me >> bit) & 1) == 0
        held = jnp.concatenate([jnp.where(low, held, got), jnp.where(low, got, held)], axis=0)
    return held


def bit_reversed(x, axis, size):
    bits = size.bit_length() - 1
    shape = x.shape[:axis] + (2,) * bits + x.shape[axis + 1:]
    order = list(range(axis)) + [axis + bits - 1 - k for k in range(bits)] + list(range(axis + bits, len(shape)))
    return x.reshape(shape).transpose(order).reshape(x.shape)


def contract(left, right):
    return lax.dot_general(
        left, right, (((0, 1, 3), (0, 1, 3)), ((), ())), preferred_element_type=jnp.float32
    )


def lag_block(background, analysis, cycle_total, max_lag, lags):
    pieces = []
    for k in lags:
        offset = k - max_lag
        if offset >= 0:
            span = cycle_total - offset
            pieces.append(contract(background[:, offset:], analysis[:, :span]))
        else:
            span = cycle_total + offset
            pieces.append(contract(background[:, :span], analysis[:, -offset:]))
    return jnp.stack(pieces, axis=1)


def body(analysis_dep, background_dep, valid_counts):
    cycle_total = valid_counts.shape[0]
    quad_size = lax.axis_size("tq")
    chan_size = lax.axis_size("chan")
    lag_total = 5
    max_lag = (lag_total - 1) // 2
    pair_index = lax.axis_index("th")
    cycle_index = lax.axis_index("tq") * PAIR + pair_index
    own_count = jnp.sum(
        jnp.where(jnp.arange(cycle_total, dtype=jnp.int32) == cycle_index, valid_counts, 0)
    )
    _, width_block, loc_total = analysis_dep.shape
    half = loc_total // PAIR
    piece = half // chan_size
    pair_rows = width_block * chan_size // quad_size
    valid_cols = (jnp.arange(loc_total, dtype=jnp.int32) < own_count)[None, :]
    local_analysis = jnp.where(valid_cols, analysis_dep[0], jnp.zeros((), jnp.bfloat16))
    local_background = jnp.where(valid_cols, background_dep[0], jnp.zeros((), jnp.bfloat16))

    low_half = local_analysis[:, :half]
    high_half = local_analysis[:, half:]
    keep = jnp.where(pair_index == 0, low_half, high_half)
    give = jnp.where(pair_index == 0, high_half, low_half)
    def by_piece(x):
        pieces_first = x.reshape(width_block, chan_size, piece).transpose(1, 0, 2)
        return bit_reversed(pieces_first, 0, chan_size)[:, None]

    same_parity = lax.all_gather(by_piece(keep), "tq", axis=1, tiled=True)
    got = swap_pair(give)
    other_parity = lax.all_gather(by_piece(got), "tq", axis=1, tiled=True)
    in_order = jnp.stack([same_parity, other_parity], axis=2)
    swapped = jnp.stack([other_parity, same_parity], axis=2)
    all_analysis = jnp.where(pair_index == 0, in_order, swapped)
    all_analysis = all_analysis.reshape(chan_size, cycle_total, width_block, piece)

    split_b = local_background.reshape(width_block, PAIR, chan_size, piece)
    by_loc = lax.all_to_all(split_b, "chan", 2, 0, tiled=True)
    by_loc = by_loc.reshape(quad_size, pair_rows, PAIR, piece).transpose(0, 2, 1, 3)
    by_loc = by_loc.reshape(quad_size * PAIR, pair_rows, piece)
    rows_here = lax.all_to_all(by_loc, ("tq", "th"), 0, 0, tiled=True)
    all_background = gather_chan(rows_here)

    rows_out = pair_rows // PAIR
    give_rows = lax.dynamic_slice_in_dim(all_background, (1 - pair_index) * rows_out, rows_out, axis=2)
    keep_rows = lax.dynamic_slice_in_dim(all_background, pair_index * rows_out, rows_out, axis=2)
    first = (0,)
    second = (lag_total - 1,)
    inner = tuple(range(1, lag_total - 1))
    first_partial = lag_block(give_rows, all_analysis, cycle_total, max_lag, first)
    first_partial, all_analysis, give_rows, keep_rows = lax.optimization_barrier(
        (first_partial, all_analysis, give_rows, keep_rows)
    )
    sent_first = swap_pair(first_partial)
    sent_second = swap_pair(lag_block(give_rows, all_analysis, cycle_total, max_lag, second))
    sent_inner = swap_pair(lag_block(give_rows, all_analysis, cycle_total, max_lag, inner))
    own = lag_block(keep_rows, all_analysis, cycle_total, max_lag, range(lag_total))
    sent = jnp.concatenate([sent_first, sent_inner, sent_second], axis=1)
    summed = own + sent

    denominators = []
    for offset in range(max_lag + 1):
        span = cycle_total - offset
        denominators.append(
            jnp.sum(jnp.minimum(valid_counts[:span], valid_counts[offset:])).astype(jnp.float32)
        )
    divisor = jnp.stack([denominators[abs(k - max_lag)] for k in range(lag_total)])
    return summed / divisor[None, :, None]


def solution(mesh):
    tm_size, chan_size = mesh.devices.shape
    split = Mesh(mesh.devices.reshape(tm_size // PAIR, PAIR, chan_size), ("tq", "th", "chan"))
    in_specs = (P(("tq", "th"), "chan", None), P(("tq", "th"), "chan", None), P())
    out_specs = P(("tq", "th"), None, "chan")
    return jax.shard_map(body, mesh=split, in_specs=in_specs, out_specs=out_specs, check_vma=False)
```

```python
import jax
import jax.numpy as jnp
from jax import lax
from jax.sharding import Mesh, PartitionSpec as P

PAIR = 2


def swap_pair(x):
    return lax.ppermute(x, "th", [(0, 1), (1, 0)])


def gather_chan(x):
    size = lax.axis_size("chan")
    me = lax.axis_index("chan")
    bits = size.bit_length() - 1
    held = x[None]
    for bit in reversed(range(bits)):
        got = lax.ppermute(held, "chan", [(c, c ^ (1 << bit)) for c in range(size)])
        low = ((me >> bit) & 1) == 0
        held = jnp.concatenate([jnp.where(low, held, got), jnp.where(low, got, held)], axis=0)
    return held


def bit_reversed(x, axis, size):
    bits = size.bit_length() - 1
    shape = x.shape[:axis] + (2,) * bits + x.shape[axis + 1:]
    order = list(range(axis)) + [axis + bits - 1 - k for k in range(bits)] + list(range(axis + bits, len(shape)))
    return x.reshape(shape).transpose(order).reshape(x.shape)


def relay_gather(block, size):
    me = lax.axis_index("tq")
    from_left = from_right = block
    lefts, rights = [], []
    for _ in range(size - 1):
        from_left = lax.ppermute(from_left, "tq", [(i, i + 1) for i in range(size - 1)])
        from_right = lax.ppermute(from_right, "tq", [(i + 1, i) for i in range(size - 1)])
        lefts.append(from_left)
        rights.append(from_right)
    stacked = jnp.concatenate(lefts[::-1] + [block] + rights, axis=1)
    width = block.shape[1]
    return lax.dynamic_slice_in_dim(stacked, (size - 1 - me) * width, size * width, axis=1)


def contract(left, right):
    return lax.dot_general(
        left, right, (((0, 1, 3), (0, 1, 3)), ((), ())), preferred_element_type=jnp.float32
    )


def lag_block(background, analysis, cycle_total, max_lag, lags):
    pieces = []
    for k in lags:
        offset = k - max_lag
        if offset >= 0:
            span = cycle_total - offset
            pieces.append(contract(background[:, offset:], analysis[:, :span]))
        else:
            span = cycle_total + offset
            pieces.append(contract(background[:, :span], analysis[:, -offset:]))
    return jnp.stack(pieces, axis=1)


def body(analysis_dep, background_dep, valid_counts):
    cycle_total = valid_counts.shape[0]
    quad_size = lax.axis_size("tq")
    chan_size = lax.axis_size("chan")
    lag_total = 5
    max_lag = (lag_total - 1) // 2
    pair_index = lax.axis_index("th")
    cycle_index = lax.axis_index("tq") * PAIR + pair_index
    own_count = jnp.sum(
        jnp.where(jnp.arange(cycle_total, dtype=jnp.int32) == cycle_index, valid_counts, 0)
    )
    _, width_block, loc_total = analysis_dep.shape
    half = loc_total // PAIR
    piece = half // chan_size
    pair_rows = width_block * chan_size // quad_size
    valid_cols = (jnp.arange(loc_total, dtype=jnp.int32) < own_count)[None, :]
    local_analysis = jnp.where(valid_cols, analysis_dep[0], jnp.zeros((), jnp.bfloat16))
    local_background = jnp.where(valid_cols, background_dep[0], jnp.zeros((), jnp.bfloat16))

    low_half = local_analysis[:, :half]
    high_half = local_analysis[:, half:]
    keep = jnp.where(pair_index == 0, low_half, high_half)
    give = jnp.where(pair_index == 0, high_half, low_half)
    def by_piece(x):
        pieces_first = x.reshape(width_block, chan_size, piece).transpose(1, 0, 2)
        return bit_reversed(pieces_first, 0, chan_size)[:, None]

    same_parity = lax.all_gather(by_piece(keep), "tq", axis=1, tiled=True)
    got = swap_pair(give)
    other_parity = relay_gather(by_piece(got), quad_size)
    in_order = jnp.stack([same_parity, other_parity], axis=2)
    swapped = jnp.stack([other_parity, same_parity], axis=2)
    all_analysis = jnp.where(pair_index == 0, in_order, swapped)
    all_analysis = all_analysis.reshape(chan_size, cycle_total, width_block, piece)

    split_b = local_background.reshape(width_block, PAIR, chan_size, piece)
    by_loc = lax.all_to_all(split_b, "chan", 2, 0, tiled=True)
    by_loc = by_loc.reshape(quad_size, pair_rows, PAIR, piece).transpose(0, 2, 1, 3)
    by_loc = by_loc.reshape(quad_size * PAIR, pair_rows, piece)
    rows_here = lax.all_to_all(by_loc, ("tq", "th"), 0, 0, tiled=True)
    all_background = gather_chan(rows_here)

    rows_out = pair_rows // PAIR
    give_rows = lax.dynamic_slice_in_dim(all_background, (1 - pair_index) * rows_out, rows_out, axis=2)
    keep_rows = lax.dynamic_slice_in_dim(all_background, pair_index * rows_out, rows_out, axis=2)
    first = (0,)
    second = (lag_total - 1,)
    inner = tuple(range(1, lag_total - 1))
    first_partial = lag_block(give_rows, all_analysis, cycle_total, max_lag, first)
    first_partial, all_analysis, give_rows, keep_rows = lax.optimization_barrier(
        (first_partial, all_analysis, give_rows, keep_rows)
    )
    sent_first = swap_pair(first_partial)
    sent_second = swap_pair(lag_block(give_rows, all_analysis, cycle_total, max_lag, second))
    sent_inner = swap_pair(lag_block(give_rows, all_analysis, cycle_total, max_lag, inner))
    own = lag_block(keep_rows, all_analysis, cycle_total, max_lag, range(lag_total))
    sent = jnp.concatenate([sent_first, sent_inner, sent_second], axis=1)
    summed = own + sent

    denominators = []
    for offset in range(max_lag + 1):
        span = cycle_total - offset
        denominators.append(
            jnp.sum(jnp.minimum(valid_counts[:span], valid_counts[offset:])).astype(jnp.float32)
        )
    divisor = jnp.stack([denominators[abs(k - max_lag)] for k in range(lag_total)])
    return summed / divisor[None, :, None]


def solution(mesh):
    tm_size, chan_size = mesh.devices.shape
    split = Mesh(mesh.devices.reshape(tm_size // PAIR, PAIR, chan_size), ("tq", "th", "chan"))
    in_specs = (P(("tq", "th"), "chan", None), P(("tq", "th"), "chan", None), P())
    out_specs = P(("tq", "th"), None, "chan")
    return jax.shard_map(body, mesh=split, in_specs=in_specs, out_specs=out_specs, check_vma=False)
```

```python
import jax
import jax.numpy as jnp
from jax import lax
from jax.sharding import Mesh, PartitionSpec as P

PAIR = 2


def swap_pair(x):
    return lax.ppermute(x, "th", [(0, 1), (1, 0)])


def gather_chan(x):
    size = lax.axis_size("chan")
    me = lax.axis_index("chan")
    bits = size.bit_length() - 1
    held = x[None]
    for bit in reversed(range(bits)):
        got = lax.ppermute(held, "chan", [(c, c ^ (1 << bit)) for c in range(size)])
        low = ((me >> bit) & 1) == 0
        held = jnp.concatenate([jnp.where(low, held, got), jnp.where(low, got, held)], axis=0)
    return held


def bit_reversed(x, axis, size):
    bits = size.bit_length() - 1
    shape = x.shape[:axis] + (2,) * bits + x.shape[axis + 1:]
    order = list(range(axis)) + [axis + bits - 1 - k for k in range(bits)] + list(range(axis + bits, len(shape)))
    return x.reshape(shape).transpose(order).reshape(x.shape)


def contract(left, right):
    return lax.dot_general(
        left, right, (((0, 1, 3), (0, 1, 3)), ((), ())), preferred_element_type=jnp.float32
    )


def lag_block(background, analysis, cycle_total, max_lag, lags):
    pieces = []
    for k in lags:
        offset = k - max_lag
        if offset >= 0:
            span = cycle_total - offset
            pieces.append(contract(background[:, offset:], analysis[:, :span]))
        else:
            span = cycle_total + offset
            pieces.append(contract(background[:, :span], analysis[:, -offset:]))
    return jnp.stack(pieces, axis=1)


def body(analysis_dep, background_dep, valid_counts):
    cycle_total = valid_counts.shape[0]
    quad_size = lax.axis_size("tq")
    chan_size = lax.axis_size("chan")
    lag_total = 5
    max_lag = (lag_total - 1) // 2
    pair_index = lax.axis_index("th")
    cycle_index = lax.axis_index("tq") * PAIR + pair_index
    own_count = jnp.sum(
        jnp.where(jnp.arange(cycle_total, dtype=jnp.int32) == cycle_index, valid_counts, 0)
    )
    _, width_block, loc_total = analysis_dep.shape
    half = loc_total // PAIR
    piece = half // chan_size
    pair_rows = width_block * chan_size // quad_size
    valid_cols = (jnp.arange(loc_total, dtype=jnp.int32) < own_count)[None, :]
    local_analysis = jnp.where(valid_cols, analysis_dep[0], jnp.zeros((), jnp.bfloat16))
    local_background = jnp.where(valid_cols, background_dep[0], jnp.zeros((), jnp.bfloat16))

    low_half = local_analysis[:, :half]
    high_half = local_analysis[:, half:]
    keep = jnp.where(pair_index == 0, low_half, high_half)
    give = jnp.where(pair_index == 0, high_half, low_half)
    def by_piece(x):
        pieces_first = x.reshape(width_block, chan_size, piece).transpose(1, 0, 2)
        return bit_reversed(pieces_first, 0, chan_size)[:, None]

    same_parity = lax.all_gather(by_piece(keep), "tq", axis=1, tiled=True)
    got = swap_pair(give)
    other_parity = lax.all_gather(by_piece(got), "tq", axis=1, tiled=True)
    in_order = jnp.stack([same_parity, other_parity], axis=2)
    swapped = jnp.stack([other_parity, same_parity], axis=2)
    all_analysis = jnp.where(pair_index == 0, in_order, swapped)
    all_analysis = all_analysis.reshape(chan_size, cycle_total, width_block, piece)

    chunks = [local_background[:, k * piece:(k + 1) * piece] for k in range(PAIR * chan_size)]
    split_b = jnp.stack(chunks, axis=0).reshape(PAIR, chan_size, width_block, piece)
    by_loc = lax.all_to_all(split_b, "chan", 1, 1, tiled=True)
    by_loc = by_loc.reshape(PAIR, quad_size, pair_rows, piece).transpose(1, 0, 2, 3)
    by_loc = by_loc.reshape(quad_size * PAIR, pair_rows, piece)
    rows_here = lax.all_to_all(by_loc, ("tq", "th"), 0, 0, tiled=True)
    all_background = gather_chan(rows_here)

    rows_out = pair_rows // PAIR
    give_rows = lax.dynamic_slice_in_dim(all_background, (1 - pair_index) * rows_out, rows_out, axis=2)
    keep_rows = lax.dynamic_slice_in_dim(all_background, pair_index * rows_out, rows_out, axis=2)
    first = (0,)
    second = (lag_total - 1,)
    inner = tuple(range(1, lag_total - 1))
    first_partial = lag_block(give_rows, all_analysis, cycle_total, max_lag, first)
    first_partial, all_analysis, give_rows, keep_rows = lax.optimization_barrier(
        (first_partial, all_analysis, give_rows, keep_rows)
    )
    sent_first = swap_pair(first_partial)
    sent_second = swap_pair(lag_block(give_rows, all_analysis, cycle_total, max_lag, second))
    sent_inner = swap_pair(lag_block(give_rows, all_analysis, cycle_total, max_lag, inner))
    own = lag_block(keep_rows, all_analysis, cycle_total, max_lag, range(lag_total))
    sent = jnp.concatenate([sent_first, sent_inner, sent_second], axis=1)
    summed = own + sent

    denominators = []
    for offset in range(max_lag + 1):
        span = cycle_total - offset
        denominators.append(
            jnp.sum(jnp.minimum(valid_counts[:span], valid_counts[offset:])).astype(jnp.float32)
        )
    divisor = jnp.stack([denominators[abs(k - max_lag)] for k in range(lag_total)])
    return summed / divisor[None, :, None]


def solution(mesh):
    tm_size, chan_size = mesh.devices.shape
    split = Mesh(mesh.devices.reshape(tm_size // PAIR, PAIR, chan_size), ("tq", "th", "chan"))
    in_specs = (P(("tq", "th"), "chan", None), P(("tq", "th"), "chan", None), P())
    out_specs = P(("tq", "th"), None, "chan")
    return jax.shard_map(body, mesh=split, in_specs=in_specs, out_specs=out_specs, check_vma=False)
```

```python
import jax
import jax.numpy as jnp
from jax import lax
from jax.sharding import Mesh, PartitionSpec as P

PAIR = 2


def swap_pair(x):
    return lax.ppermute(x, "th", [(0, 1), (1, 0)])


def gather_chan(x):
    size = lax.axis_size("chan")
    me = lax.axis_index("chan")
    bits = size.bit_length() - 1
    held = x[None]
    for bit in reversed(range(bits)):
        got = lax.ppermute(held, "chan", [(c, c ^ (1 << bit)) for c in range(size)])
        low = ((me >> bit) & 1) == 0
        held = jnp.concatenate([jnp.where(low, held, got), jnp.where(low, got, held)], axis=0)
    return held


def bit_reversed(x, axis, size):
    bits = size.bit_length() - 1
    shape = x.shape[:axis] + (2,) * bits + x.shape[axis + 1:]
    order = list(range(axis)) + [axis + bits - 1 - k for k in range(bits)] + list(range(axis + bits, len(shape)))
    return x.reshape(shape).transpose(order).reshape(x.shape)


def contract(left, right):
    return lax.dot_general(
        left, right, (((0, 1, 3), (0, 1, 3)), ((), ())), preferred_element_type=jnp.float32
    )


def lag_block(background, analysis, cycle_total, max_lag, lags):
    pieces = []
    for k in lags:
        offset = k - max_lag
        if offset >= 0:
            span = cycle_total - offset
            pieces.append(contract(background[:, offset:], analysis[:, :span]))
        else:
            span = cycle_total + offset
            pieces.append(contract(background[:, :span], analysis[:, -offset:]))
    return jnp.stack(pieces, axis=1)


def body(analysis_dep, background_dep, valid_counts):
    cycle_total = valid_counts.shape[0]
    quad_size = lax.axis_size("tq")
    chan_size = lax.axis_size("chan")
    lag_total = 5
    max_lag = (lag_total - 1) // 2
    pair_index = lax.axis_index("th")
    cycle_index = lax.axis_index("tq") * PAIR + pair_index
    own_count = jnp.sum(
        jnp.where(jnp.arange(cycle_total, dtype=jnp.int32) == cycle_index, valid_counts, 0)
    )
    _, width_block, loc_total = analysis_dep.shape
    half = loc_total // PAIR
    piece = half // chan_size
    pair_rows = width_block * chan_size // quad_size
    valid_cols = (jnp.arange(loc_total, dtype=jnp.int32) < own_count)[None, :]
    local_analysis = jnp.where(valid_cols, analysis_dep[0], jnp.zeros((), jnp.bfloat16))
    local_background = jnp.where(valid_cols, background_dep[0], jnp.zeros((), jnp.bfloat16))

    keep = lax.dynamic_slice_in_dim(local_analysis, pair_index * half, half, axis=1)
    give = lax.dynamic_slice_in_dim(local_analysis, (1 - pair_index) * half, half, axis=1)
    def by_piece(x):
        pieces_first = x.reshape(width_block, chan_size, piece).transpose(1, 0, 2)
        return bit_reversed(pieces_first, 0, chan_size)[:, None]

    same_parity = lax.all_gather(by_piece(keep), "tq", axis=1, tiled=True)
    got = swap_pair(give)
    other_parity = lax.all_gather(by_piece(got), "tq", axis=1, tiled=True)
    in_order = jnp.stack([same_parity, other_parity], axis=2)
    swapped = jnp.stack([other_parity, same_parity], axis=2)
    all_analysis = jnp.where(pair_index == 0, in_order, swapped)
    all_analysis = all_analysis.reshape(chan_size, cycle_total, width_block, piece)

    split_b = local_background.reshape(width_block, PAIR, chan_size, piece)
    by_loc = lax.all_to_all(split_b, "chan", 2, 0, tiled=True)
    by_loc = by_loc.reshape(quad_size, pair_rows, PAIR, piece).transpose(0, 2, 1, 3)
    by_loc = by_loc.reshape(quad_size * PAIR, pair_rows, piece)
    rows_here = lax.all_to_all(by_loc, ("tq", "th"), 0, 0, tiled=True)
    all_background = gather_chan(rows_here)

    rows_out = pair_rows // PAIR
    give_rows = lax.dynamic_slice_in_dim(all_background, (1 - pair_index) * rows_out, rows_out, axis=2)
    keep_rows = lax.dynamic_slice_in_dim(all_background, pair_index * rows_out, rows_out, axis=2)
    first = (0,)
    second = (lag_total - 1,)
    inner = tuple(range(1, lag_total - 1))
    first_partial = lag_block(give_rows, all_analysis, cycle_total, max_lag, first)
    first_partial, all_analysis, give_rows, keep_rows = lax.optimization_barrier(
        (first_partial, all_analysis, give_rows, keep_rows)
    )
    sent_first = swap_pair(first_partial)
    sent_second = swap_pair(lag_block(give_rows, all_analysis, cycle_total, max_lag, second))
    sent_inner = swap_pair(lag_block(give_rows, all_analysis, cycle_total, max_lag, inner))
    own = lag_block(keep_rows, all_analysis, cycle_total, max_lag, range(lag_total))
    sent = jnp.concatenate([sent_first, sent_inner, sent_second], axis=1)
    summed = own + sent

    denominators = []
    for offset in range(max_lag + 1):
        span = cycle_total - offset
        denominators.append(
            jnp.sum(jnp.minimum(valid_counts[:span], valid_counts[offset:])).astype(jnp.float32)
        )
    divisor = jnp.stack([denominators[abs(k - max_lag)] for k in range(lag_total)])
    return summed / divisor[None, :, None]


def solution(mesh):
    tm_size, chan_size = mesh.devices.shape
    split = Mesh(mesh.devices.reshape(tm_size // PAIR, PAIR, chan_size), ("tq", "th", "chan"))
    in_specs = (P(("tq", "th"), "chan", None), P(("tq", "th"), "chan", None), P())
    out_specs = P(("tq", "th"), None, "chan")
    return jax.shard_map(body, mesh=split, in_specs=in_specs, out_specs=out_specs, check_vma=False)
```

```python
import jax
import jax.numpy as jnp
from jax import lax
from jax.sharding import Mesh, PartitionSpec as P

PAIR = 2


def swap_pair(x):
    return lax.ppermute(x, "th", [(0, 1), (1, 0)])


def gather_chan(x):
    size = lax.axis_size("chan")
    me = lax.axis_index("chan")
    bits = size.bit_length() - 1
    held = x[None]
    for bit in reversed(range(bits)):
        got = lax.ppermute(held, "chan", [(c, c ^ (1 << bit)) for c in range(size)])
        low = ((me >> bit) & 1) == 0
        held = jnp.concatenate([jnp.where(low, held, got), jnp.where(low, got, held)], axis=0)
    return held


def bit_reversed(x, axis, size):
    bits = size.bit_length() - 1
    shape = x.shape[:axis] + (2,) * bits + x.shape[axis + 1:]
    order = list(range(axis)) + [axis + bits - 1 - k for k in range(bits)] + list(range(axis + bits, len(shape)))
    return x.reshape(shape).transpose(order).reshape(x.shape)


def contract(left, right):
    return lax.dot_general(
        left, right, (((0, 1, 3), (0, 1, 3)), ((), ())), preferred_element_type=jnp.float32
    )


def lag_block(background, analysis, cycle_total, max_lag, lags):
    pieces = []
    for k in lags:
        offset = k - max_lag
        if offset >= 0:
            span = cycle_total - offset
            pieces.append(contract(background[:, offset:], analysis[:, :span]))
        else:
            span = cycle_total + offset
            pieces.append(contract(background[:, :span], analysis[:, -offset:]))
    return jnp.stack(pieces, axis=1)


def body(analysis_dep, background_dep, valid_counts):
    cycle_total = valid_counts.shape[0]
    quad_size = lax.axis_size("tq")
    chan_size = lax.axis_size("chan")
    lag_total = 5
    max_lag = (lag_total - 1) // 2
    pair_index = lax.axis_index("th")
    cycle_index = lax.axis_index("tq") * PAIR + pair_index
    own_count = jnp.sum(
        jnp.where(jnp.arange(cycle_total, dtype=jnp.int32) == cycle_index, valid_counts, 0)
    )
    _, width_block, loc_total = analysis_dep.shape
    half = loc_total // PAIR
    piece = half // chan_size
    pair_rows = width_block * chan_size // quad_size
    valid_cols = (jnp.arange(loc_total, dtype=jnp.int32) < own_count)[None, :]
    local_analysis = jnp.where(valid_cols, analysis_dep[0], jnp.zeros((), jnp.bfloat16))
    local_background = jnp.where(valid_cols, background_dep[0], jnp.zeros((), jnp.bfloat16))

    low_half = local_analysis[:, :half]
    high_half = local_analysis[:, half:]
    keep = jnp.where(pair_index == 0, low_half, high_half)
    give = jnp.where(pair_index == 0, high_half, low_half)
    def by_piece(x):
        pieces_first = x.reshape(width_block, chan_size, piece).transpose(1, 0, 2)
        return bit_reversed(pieces_first, 0, chan_size)[:, None]

    same_parity = lax.all_gather(by_piece(keep), "tq", axis=1, tiled=True)
    got = swap_pair(give)
    other_parity = lax.all_gather(by_piece(got), "tq", axis=1, tiled=True)
    all_analysis = lax.cond(
        pair_index == 0,
        lambda a, b: jnp.stack([a, b], axis=2),
        lambda a, b: jnp.stack([b, a], axis=2),
        same_parity,
        other_parity,
    )
    all_analysis = all_analysis.reshape(chan_size, cycle_total, width_block, piece)

    split_b = local_background.reshape(width_block, PAIR, chan_size, piece)
    by_loc = lax.all_to_all(split_b, "chan", 2, 0, tiled=True)
    by_loc = by_loc.reshape(quad_size, pair_rows, PAIR, piece).transpose(0, 2, 1, 3)
    by_loc = by_loc.reshape(quad_size * PAIR, pair_rows, piece)
    rows_here = lax.all_to_all(by_loc, ("tq", "th"), 0, 0, tiled=True)
    all_background = gather_chan(rows_here)

    rows_out = pair_rows // PAIR
    give_rows = lax.dynamic_slice_in_dim(all_background, (1 - pair_index) * rows_out, rows_out, axis=2)
    keep_rows = lax.dynamic_slice_in_dim(all_background, pair_index * rows_out, rows_out, axis=2)
    first = (0,)
    second = (lag_total - 1,)
    inner = tuple(range(1, lag_total - 1))
    first_partial = lag_block(give_rows, all_analysis, cycle_total, max_lag, first)
    first_partial, all_analysis, give_rows, keep_rows = lax.optimization_barrier(
        (first_partial, all_analysis, give_rows, keep_rows)
    )
    sent_first = swap_pair(first_partial)
    sent_second = swap_pair(lag_block(give_rows, all_analysis, cycle_total, max_lag, second))
    sent_inner = swap_pair(lag_block(give_rows, all_analysis, cycle_total, max_lag, inner))
    own = lag_block(keep_rows, all_analysis, cycle_total, max_lag, range(lag_total))
    sent = jnp.concatenate([sent_first, sent_inner, sent_second], axis=1)
    summed = own + sent

    denominators = []
    for offset in range(max_lag + 1):
        span = cycle_total - offset
        denominators.append(
            jnp.sum(jnp.minimum(valid_counts[:span], valid_counts[offset:])).astype(jnp.float32)
        )
    divisor = jnp.stack([denominators[abs(k - max_lag)] for k in range(lag_total)])
    return summed / divisor[None, :, None]


def solution(mesh):
    tm_size, chan_size = mesh.devices.shape
    split = Mesh(mesh.devices.reshape(tm_size // PAIR, PAIR, chan_size), ("tq", "th", "chan"))
    in_specs = (P(("tq", "th"), "chan", None), P(("tq", "th"), "chan", None), P())
    out_specs = P(("tq", "th"), None, "chan")
    return jax.shard_map(body, mesh=split, in_specs=in_specs, out_specs=out_specs, check_vma=False)
```
